512 devices in a mesh: lon: 64 (over z, x), lat: 8 (over y, core).
Axes of the slice: x: 4, y: 4, z: 16, core: 2. Of those that a mesh axis runs over, the one named last changes fastest.
Arguments:
- wet_mask: int32 [4096, 8192], P('lat', 'lon'), may hold values 0 or 1
- east_level: int32 [4096, 8192], P('lat', 'lon'), may hold values from 0 to 8
- north_level: int32 [4096, 8192], P('lat', 'lon'), may hold values from 0 to 8, as said below
- courant: float32 [4096, 8192], P('lat', 'lon'), may hold values from 0.1 to 0.45
- increment: float32 [4096, 8192], P('lat', 'lon'), may hold values from -6 to 6
- innovation: float32 [4096, 8192], P('lat', 'lon'), may hold values from -6 to 6
- obs_weight: float32 [4096, 8192], P('lat', 'lon'), may hold values from 0.2 to 2
- smooth_scale: float32 [4096], P('lat'), may hold values from 2.5 to 10
Outputs:
- final_eta: float32 [4096, 8192], P('lat', 'lon')
- precond_grad: float32 [4096, 8192], P('lat', 'lon')
The draws below stay inside these ranges and needn't reach their ends.
Inputs may be any that keep to these rules, and one draw needn't show every extreme that they name: `north_level`: on the top row every north face is open at least half of 8 levels.
All inputs are finite; a program needn't handle non-finite values. No bound on the sum of `wet_mask` on one device may be relied on, other than what follows from the above.
Results may differ from the reference program's by a relative error of at most 0.00023.
Values sent between devices are 32-bit elements; how exact they have to be, the bound alone decides.
A program may use at most 64 MiB of HBM per device.

```python
import math
import jax
import jax.numpy as jnp

CLON = 128
SUBSTEPS = 4
WLEV = 8
NLAT = 4096
NLON = 8192


def draw_innovation(key, part):
    shape = (NLAT, NLON)
    values = jax.random.normal(key, shape, jnp.float32)
    return jnp.clip(values, -6.0, 6.0)


def draw_north_level(key, part):
    shape = (NLAT, NLON)
    lower = jax.random.randint(jax.random.fold_in(key, 11), shape, 0, WLEV + 1)
    upper = jax.random.randint(jax.random.fold_in(key, 12), shape, WLEV // 2, WLEV + 1)
    row_index = jnp.arange(NLAT, dtype=jnp.int32)[:, None]
    return jnp.where(row_index == NLAT - 1, upper, lower).astype(jnp.int32)


def set_ends(drawn, stream_key, least, high):
    longest = drawn.shape.index(max(drawn.shape))
    spots = []
    for shift in (0, 1):
        where = [jax.random.randint(jax.random.fold_in(stream_key, axis), (), 0, length) for axis, length in enumerate(drawn.shape)]
        where[longest] = (where[longest] + shift) % drawn.shape[longest]
        spots.append(tuple(where))
    return drawn.at[spots[0]].set(least).at[spots[1]].set(high)


def levels(stream_key, dims, split, least, high):
    level, own = 1.0, jax.random.fold_in(stream_key, 6)
    for position, parts in split:
        draws = jnp.exp(jax.random.uniform(jax.random.fold_in(own, position), (parts,), jnp.float32, least / len(split), high / len(split)))
        level = level * jnp.repeat(draws, dims[position] // parts).reshape([-1 if axis == position else 1 for axis in range(len(dims))])
    return level


def gaussian(rng, dims, scale, bound, cuts=(), kind=jnp.bfloat16):
    values = jax.random.normal(rng, dims, jnp.float32) * scale
    if len(cuts) > 0:
        values = levels(rng, dims, cuts, -0.22, 0.18) * values
    return jnp.clip(values, min=-bound, max=bound).astype(kind)


def setup_inputs(seed: int = 0) -> dict:
    arg_keys = jax.random.split(jax.random.key(seed), 9)
    wet_mask = set_ends((jax.random.randint(arg_keys[0], (NLAT, NLON), 0, 5) < 4).astype(jnp.int32), jax.random.fold_in(arg_keys[0], 1), 0, 1)
    east_level = set_ends(jax.random.randint(arg_keys[1], (NLAT, NLON), 0, WLEV + 1), jax.random.fold_in(arg_keys[1], 1), 0, WLEV).astype(jnp.int32)
    north_level = draw_north_level(jax.random.fold_in(arg_keys[8], 71), 0)
    courant = jnp.clip(0.1 + 0.35 * jax.random.uniform(arg_keys[3], (NLAT, NLON), jnp.float32) ** levels(arg_keys[3], (NLAT, NLON), ((0, 8), (1, 64)), -0.2, 0.2), 0.1, 0.45)
    increment = gaussian(arg_keys[4], (NLAT, NLON), 1.0, 6.0, ((0, 8), (1, 64)), jnp.float32)
    innovation = draw_innovation(jax.random.fold_in(arg_keys[8], 71), 0)
    obs_weight = jnp.clip(jnp.exp(math.log(2.0) - 2.3025851 * jax.random.uniform(arg_keys[6], (NLAT, NLON), jnp.float32) ** levels(arg_keys[6], (NLAT, NLON), ((0, 8), (1, 64)), -0.2, 0.2)), 0.2, 2.0)
    smooth_scale = jnp.clip(jnp.exp(math.log(10.0) - 1.3862944 * jax.random.uniform(arg_keys[7], (NLAT,), jnp.float32) ** levels(arg_keys[7], (NLAT,), ((0, 8),), -0.2, 0.2)), 2.5, 10.0)
    return dict(wet_mask=wet_mask, east_level=east_level, north_level=north_level, courant=courant, increment=increment, innovation=innovation, obs_weight=obs_weight, smooth_scale=smooth_scale)


def periodic_solve(source, stiffness):
    width = source.shape[1]
    stiff_rows = stiffness[:, None]
    root_term = jnp.sqrt(1.0 + 4.0 * stiff_rows)
    log_root = jnp.log1p(-(root_term - 1.0) / (2.0 * stiff_rows))
    green_scale = 1.0 / root_term
    forward_sum = source
    backward_sum = source
    stride = 1
    while stride < width:
        factor = jnp.exp(float(stride) * log_root)
        forward_sum = forward_sum + factor * jnp.pad(forward_sum[:, :-stride], ((0, 0), (stride, 0)))
        backward_sum = backward_sum + factor * jnp.pad(backward_sum[:, stride:], ((0, 0), (0, stride)))
        stride = stride * 2
    image_sum = 1.0 - jnp.exp(float(width) * log_root)
    east_in = forward_sum[:, -1:] / image_sum
    west_in = backward_sum[:, :1] / image_sum
    column = jnp.arange(width, dtype=jnp.float32)[None, :]
    forward_all = forward_sum + jnp.exp((column + 1.0) * log_root) * east_in
    backward_all = backward_sum + jnp.exp((float(width) - column) * log_root) * west_in
    return green_scale * (forward_all + backward_all - source)

def reference(wet_mask, east_level, north_level, courant, increment, innovation, obs_weight, smooth_scale):
    wet_frac = wet_mask.astype(jnp.float32)
    east_face = east_level.astype(jnp.float32) / WLEV
    raw_north = north_level.astype(jnp.float32) / WLEV
    west_face = jnp.roll(east_face, 1, axis=1)
    fold_face = raw_north[-1] * raw_north[-1, ::-1]
    north_face = jnp.concatenate([raw_north[:-1], fold_face[None]], axis=0)
    south_face = jnp.concatenate([jnp.zeros_like(raw_north[:1]), raw_north[:-1]], axis=0)

    def laplace(state_now):
        north_vals = jnp.concatenate([state_now[1:], state_now[-1:, ::-1]], axis=0)
        south_vals = jnp.concatenate([jnp.zeros_like(state_now[:1]), state_now[:-1]], axis=0)
        return east_face * (jnp.roll(state_now, -1, axis=1) - state_now) + west_face * (jnp.roll(state_now, 1, axis=1) - state_now) + north_face * (north_vals - state_now) + south_face * (south_vals - state_now)
    state_now = wet_frac * increment
    before = state_now
    for substep in range(SUBSTEPS):
        after = 2.0 * state_now - before + wet_frac * courant * laplace(state_now)
        before = state_now
        state_now = after
    final_eta = state_now
    adjoint = wet_frac * obs_weight * (state_now - innovation)
    carried = jnp.zeros_like(adjoint)
    for substep in range(SUBSTEPS):
        updated = 2.0 * adjoint + wet_frac * laplace(courant * wet_frac * adjoint) + carried
        carried = -adjoint
        adjoint = updated
    gradient = wet_frac * (adjoint + carried)
    stiffness = smooth_scale * float(CLON * CLON)
    smoothed = periodic_solve(gradient, stiffness) * (2.0 * stiffness ** 0.25)[:, None]
    return (final_eta, smoothed)
```

```python
import functools
import jax
import jax.numpy as jnp
from jax import lax
from jax.experimental import pallas as pl
from jax.experimental.pallas import tpu as pltpu
from jax.sharding import PartitionSpec as P

SUBSTEPS = 4
WLEV = 8
F32 = jnp.float32
BF16 = jnp.bfloat16
XG = 4
FIELDS = 6
PAD = 16
RH = 48
HIGH = lax.Precision.HIGHEST


def roll(value, shift, axis):
    return pltpu.roll(value, shift % value.shape[axis], axis)


def iota(shape, dim):
    return lax.broadcasted_iota(jnp.int32, shape, dim)


def split3(value):
    high = value.astype(BF16)
    rest = value - high.astype(F32)
    mid = rest.astype(BF16)
    low = (rest - mid.astype(F32)).astype(BF16)
    return high, mid, low


def remote(src, dst, send_sem, recv_sem, lon, lat):
    return pltpu.make_async_remote_copy(
        src_ref=src,
        dst_ref=dst,
        send_sem=send_sem,
        recv_sem=recv_sem,
        device_id={"lon": lon, "lat": lat},
        device_id_type=pl.DeviceIdType.MESH,
    )


def kernel(
    nlon,
    nlat,
    wet_hbm,
    east_hbm,
    north_hbm,
    cour_hbm,
    incr_hbm,
    innov_hbm,
    ow_hbm,
    scale_ref,
    eta_hbm,
    grad_hbm,
    raw_i,
    raw_f,
    main,
    halo,
    work,
    delta,
    packed,
    strip_out,
    strip_in,
    corner,
    eta_buf,
    grad_buf,
    powers,
    gains,
    parts,
    sums,
    xbuf,
    zbuf,
    in_sem,
    out_sem,
    hs,
    hr,
    xs,
    xr,
    zs,
    zr,
):
    lon = lax.axis_index("lon")
    lat = lax.axis_index("lat")
    nz = nlon // XG
    x_pos = lax.rem(lon, XG)
    z_pos = lon // XG
    top = lat == nlat - 1
    low = lat == 0
    east_lon = lax.rem(lon + 1, nlon)
    west_lon = lax.rem(lon + nlon - 1, nlon)
    fold_lon = nlon - 1 - lon
    fold_ne = lax.rem(2 * nlon - 2 - lon, nlon)
    fold_nw = lax.rem(nlon - lon, nlon)
    ne_self = fold_ne == lon
    nw_self = fold_nw == lon

    loads = [
        pltpu.make_async_copy(wet_hbm, raw_i.at[0], in_sem.at[0]),
        pltpu.make_async_copy(cour_hbm, raw_f.at[0], in_sem.at[1]),
        pltpu.make_async_copy(incr_hbm, raw_f.at[1], in_sem.at[2]),
        pltpu.make_async_copy(east_hbm, raw_i.at[1], in_sem.at[3]),
        pltpu.make_async_copy(north_hbm, raw_i.at[2], in_sem.at[4]),
        pltpu.make_async_copy(ow_hbm, main.at[4, pl.ds(PAD, 512)], in_sem.at[5]),
        pltpu.make_async_copy(innov_hbm, main.at[5, pl.ds(PAD, 512)], in_sem.at[6]),
    ]
    for load in loads:
        load.start()

    barrier = pltpu.get_barrier_semaphore()

    def greet(to_lon, to_lat):
        pl.semaphore_signal(
            barrier,
            inc=1,
            device_id={"lon": to_lon, "lat": to_lat},
            device_id_type=pl.DeviceIdType.MESH,
        )

    def x_peer(step):
        return z_pos * XG + lax.rem(x_pos + step, XG)

    def z_peer(step):
        return lax.rem(z_pos + step, nz) * XG + x_pos

    greet(east_lon, lat)
    greet(west_lon, lat)

    @pl.when(jnp.logical_not(low))
    def _():
        greet(lon, lat - 1)
        greet(east_lon, lat - 1)
        greet(west_lon, lat - 1)

    @pl.when(jnp.logical_not(top))
    def _():
        greet(lon, lat + 1)
        greet(east_lon, lat + 1)
        greet(west_lon, lat + 1)

    @pl.when(top)
    def _():
        greet(fold_lon, lat)

        @pl.when(jnp.logical_not(ne_self))
        def _():
            greet(fold_ne, lat)

        @pl.when(jnp.logical_not(nw_self))
        def _():
            greet(fold_nw, lat)

    for step in range(1, XG):
        greet(x_peer(step), lat)
    for step in range(1, nz):
        greet(z_peer(step), lat)

    lane8 = iota((8, 128), 1)
    sub8 = iota((8, 128), 0)

    zero8 = jnp.zeros((8, 128), F32)
    zstrip = jnp.zeros((8, 512), F32)
    strip_in[0, 0] = zstrip
    strip_in[6, 1] = zstrip
    strip_in[7, 0] = zstrip
    strip_in[7, 1] = zstrip
    for edge in (0, 536):
        for field in (0, 3):
            main[field, pl.ds(edge, 8)] = zero8
            halo[field, pl.ds(edge, 8)] = zero8
        work[0, pl.ds(edge, 8)] = zero8
        work[1, pl.ds(edge, 8)] = zero8

    @pl.when(low)
    def _():
        for field in range(FIELDS):
            main[field, pl.ds(8, 8)] = zero8
        corner[0] = zero8
        corner[1] = zero8

    for load in loads:
        load.wait()
    slot = (iota((64, 128), 1) + 8) // 16

    def build(step, carry):
        row = pl.multiple_of(step * 64, 64)
        own = pl.ds(pl.multiple_of(step * 64 + PAD, 16), 64)
        rows = pl.ds(row, 64)
        wet = raw_i[0, rows].astype(F32)
        fields = [
            wet * raw_f[1, rows],
            wet * raw_f[0, rows],
            raw_i[1, rows].astype(F32) * (1.0 / WLEV),
            raw_i[2, rows].astype(F32) * (1.0 / WLEV),
        ]
        for index, value in enumerate(fields):
            main[index, own] = value
        fields.append(main[4, own])
        fields.append(main[5, own])
        joined = roll(fields[0], 16, 1)
        for index in range(1, FIELDS):
            joined = jnp.where(slot == index + 1, roll(fields[index], 16 * (index + 1), 1), joined)
        packed[rows] = joined
        return carry

    lax.fori_loop(0, 8, build, 0)

    def turn(step, carry):
        rows = pl.ds(pl.multiple_of(step * 128, 128), 128)
        strip_out[:, :, :, rows] = packed[rows].T.reshape(8, 2, 8, 128)
        return carry

    lax.fori_loop(0, 4, turn, 0)

    links = 2 + (XG - 1) + (nz - 1)
    north_links = jnp.where(
        top, 3 - ne_self.astype(jnp.int32) - nw_self.astype(jnp.int32), 3
    )
    south_links = jnp.where(low, 0, 3)
    pl.semaphore_wait(barrier, links + north_links + south_links)

    top_rows = main.at[:, pl.ds(PAD + 504, 8)]
    low_rows = main.at[:, pl.ds(PAD, 8)]
    south_halo = main.at[:, pl.ds(8, 8)]
    north_halo = main.at[:, pl.ds(PAD + 512, 8)]
    top_tile = packed.at[pl.ds(504, 8)]
    low_tile = packed.at[pl.ds(0, 8)]
    to_west = remote(
        strip_out.at[pl.ds(1, 6), 0], strip_in.at[pl.ds(1, 6), 0], hs.at[2], hr.at[3], west_lon, lat
    )
    to_east = remote(
        strip_out.at[pl.ds(0, 6), 1], strip_in.at[pl.ds(0, 6), 1], hs.at[3], hr.at[2], east_lon, lat
    )
    to_south = remote(low_rows, north_halo, hs.at[0], hr.at[1], lon, lat - 1)
    to_sw = remote(low_tile, corner.at[3], hs.at[4], hr.at[7], west_lon, lat - 1)
    to_se = remote(low_tile, corner.at[2], hs.at[5], hr.at[6], east_lon, lat - 1)
    to_north = remote(top_rows, south_halo, hs.at[1], hr.at[0], lon, lat + 1)
    to_nw = remote(top_tile, corner.at[1], hs.at[6], hr.at[5], west_lon, lat + 1)
    to_ne = remote(top_tile, corner.at[0], hs.at[7], hr.at[4], east_lon, lat + 1)
    over_fold = remote(top_rows, north_halo, hs.at[1], hr.at[1], fold_lon, lat)
    fold_to_nw = remote(top_tile, corner.at[2], hs.at[6], hr.at[6], fold_nw, lat)
    fold_to_ne = remote(top_tile, corner.at[3], hs.at[7], hr.at[7], fold_ne, lat)
    own_nw = pltpu.make_async_copy(top_tile, corner.at[2], hr.at[6])
    own_ne = pltpu.make_async_copy(top_tile, corner.at[3], hr.at[7])

    to_west.start()
    to_east.start()

    @pl.when(top)
    def _():
        over_fold.start()

        @pl.when(jnp.logical_not(nw_self))
        def _():
            fold_to_nw.start()

        @pl.when(nw_self)
        def _():
            own_nw.start()

        @pl.when(jnp.logical_not(ne_self))
        def _():
            fold_to_ne.start()

        @pl.when(ne_self)
        def _():
            own_ne.start()

    @pl.when(jnp.logical_not(top))
    def _():
        to_north.start()
        to_nw.start()
        to_ne.start()

    @pl.when(jnp.logical_not(low))
    def _():
        to_south.start()
        to_sw.start()
        to_se.start()

    scale = scale_ref[...]
    scale = jnp.concatenate([scale, scale], axis=0)
    stiff = scale * float(128 * 128)
    root_term = jnp.sqrt(1.0 + 4.0 * stiff)
    log_root = jnp.log1p(-(root_term - 1.0) / (2.0 * stiff))
    gain = (1.0 / root_term) * (2.0 * jnp.sqrt(jnp.sqrt(stiff)))
    both = jnp.where(sub8 < 4, log_root, gain)
    columns = jnp.concatenate([both] * 16, axis=0).T
    place = iota((128, 128), 1).astype(F32) - 63.5
    for block in range(4):
        rows = pl.ds(block * 128, 128)
        power = jnp.broadcast_to(columns[:, block : block + 1], (128, 128)) * place
        gain_rows = jnp.broadcast_to(columns[:, block + 4 : block + 5], (128, 128))
        up = jnp.exp(power)
        down = jnp.exp(-power)
        powers[rows, 0:128] = down
        powers[rows, 128:256] = up
        gains[rows, 0:128] = gain_rows * up
        gains[rows, 128:256] = gain_rows * down
    log_block = log_root * 128.0
    block_decay = jnp.exp(log_block)
    group_decay = jnp.exp(log_block * float(XG))
    image_sum = 1.0 - jnp.exp(log_block * float(nlon))

    def zero_delta(step, carry):
        rows = pl.ds(pl.multiple_of(8 + step * RH, 8), RH)
        delta[0, rows] = jnp.zeros((RH, 128), F32)
        delta[1, rows] = jnp.zeros((RH, 128), F32)
        return carry

    lax.fori_loop(0, 528 // RH, zero_delta, 0)

    first_half = lax.rem(lane8, 16) < 8
    to_east.wait_recv()
    to_west.wait_recv()

    def unturn(step, carry):
        rows = pl.ds(pl.multiple_of(step * 128, 128), 128)
        own = pl.ds(pl.multiple_of(step * 128 + PAD, 16), 128)
        edges = strip_in[:, :, :, rows].reshape(128, 128).T
        for field in range(FIELDS):
            halo[field, own] = roll(edges, -16 * (field + 1), 1)
        return carry

    lax.fori_loop(0, 4, unturn, 0)

    @pl.when(jnp.logical_not(low))
    def _():
        to_north.wait_recv()
        to_nw.wait_recv()
        to_ne.wait_recv()

    south_corner = jnp.where(first_half, corner[1], corner[0])
    for field in range(FIELDS):
        halo[field, pl.ds(8, 8)] = roll(south_corner, -16 * (field + 1), 1)
    to_south.wait_recv()
    to_sw.wait_recv()
    to_se.wait_recv()

    @pl.when(top)
    def _():
        over_fold.wait_send()

    @pl.when(jnp.logical_not(top))
    def _():
        to_north.wait_send()

    @pl.when(jnp.logical_not(low))
    def _():
        to_south.wait_send()

    @pl.when(jnp.logical_not(top))
    def _():
        north_corner = jnp.where(first_half, corner[3], corner[2])
        for field in range(FIELDS):
            halo[field, pl.ds(PAD + 512, 8)] = roll(north_corner, -16 * (field + 1), 1)

    @pl.when(top)
    def _():
        mixed = jnp.where(first_half, corner[2], corner[3])
        tiles = [main[field, pl.ds(PAD + 512, 8)] for field in range(FIELDS)] + [mixed, zero8]
        stack = jnp.concatenate(tiles, axis=0)
        flip = (iota((128, 128), 0) + iota((128, 128), 1) == 127).astype(F32)
        row_to = iota((64, 64), 0)
        row_from = iota((64, 64), 1)
        swap = (row_to // 8 == row_from // 8) & (row_to % 8 + row_from % 8 == 7)
        turned = jnp.dot(stack, flip, precision=HIGH, preferred_element_type=F32)
        turned = jnp.dot(swap.astype(F32), turned, precision=HIGH, preferred_element_type=F32)
        ghost = pl.ds(PAD + 512, 8)
        for field in range(FIELDS):
            inner = turned[8 * field : 8 * field + 8]
            outer = roll(turned[48:56], 16 * (field + 1), 1)
            if field == 2:
                inner, outer = roll(inner, -1, 1), roll(outer, -1, 1)
                inner, outer = (
                    jnp.where(lane8 == 127, outer, inner),
                    jnp.where(lane8 == 127, inner, outer),
                )
            if field == 3:
                last = pl.ds(PAD + 504, 8)
                main[3, last] = jnp.where(sub8 == 7, main[3, last] * inner[0:1], main[3, last])
                halo[3, last] = jnp.where(sub8 == 7, halo[3, last] * outer[0:1], halo[3, last])
                inner, outer = roll(inner, -1, 0), roll(outer, -1, 0)
            main[field, ghost] = inner
            halo[field, ghost] = outer

    last_lane = iota((RH, 128), 1) == 127
    zero_lane = iota((RH, 128), 1) == 0

    def substep(src, dst):
        def rows_of(step, carry):
            row = pl.multiple_of(8 + step * RH, 8)
            here = pl.ds(row, RH)
            wide = pl.ds(row - 8, RH + 16)

            def meridional(state, field):
                values = state[wide]
                face = field[3, wide]
                flux = face * (roll(values, -1, 0) - values)
                return (flux - roll(flux, 1, 0))[8 : RH + 8]

            s_in, s_out = src[0][here], src[1][here]
            e_in, e_out = roll(s_in, -1, 1), roll(s_out, -1, 1)
            f_in = main[2, here] * (jnp.where(last_lane, e_out, e_in) - s_in)
            f_out = halo[2, here] * (jnp.where(last_lane, e_in, e_out) - s_out)
            w_in, w_out = roll(f_in, 1, 1), roll(f_out, 1, 1)
            l_in = f_in - jnp.where(zero_lane, w_out, w_in) + meridional(src[0], main)
            l_out = f_out - jnp.where(zero_lane, w_in, w_out) + meridional(src[1], halo)
            d_in = delta[0, here] + main[1, here] * l_in
            d_out = delta[1, here] + halo[1, here] * l_out
            delta[0, here] = d_in
            delta[1, here] = d_out
            dst[0][here] = s_in + d_in
            dst[1][here] = s_out + d_out
            return carry

        lax.fori_loop(0, 528 // RH, rows_of, 0)

    side_a = (main.at[0], halo.at[0])
    side_b = (work.at[0], work.at[1])

    def forward_pair(step, carry):
        substep(side_a, side_b)
        substep(side_b, side_a)
        return carry

    lax.fori_loop(0, SUBSTEPS // 2, forward_pair, 0)

    def misfit(step, carry):
        here = pl.ds(pl.multiple_of(8 + step * RH, 8), RH)
        for side, field in enumerate((main, halo)):
            start = field[1, here] * field[4, here] * (field[0, here] - field[5, here])
            work[side, here] = start
            delta[side, here] = start
        return carry

    lax.fori_loop(0, 528 // RH, misfit, 0)
    eta_buf[...] = main[0, pl.ds(PAD, 512)]
    eta_out = pltpu.make_async_copy(eta_buf, eta_hbm, out_sem.at[0])
    eta_out.start()

    def adjoint_pair(step, carry):
        substep(side_b, side_a)
        substep(side_a, side_b)
        return carry

    lax.fori_loop(0, SUBSTEPS // 2, adjoint_pair, 0)

    ends = jnp.zeros((8, 128), F32)
    pick_row = iota((8, 256), 0)
    pick_half = 4 * (iota((8, 256), 1) // 128)
    for block in range(4):
        rows = pl.ds(block * 128, 128)
        gradient = delta[0, pl.ds(PAD + block * 128, 128)] / raw_f[0, rows]
        both_ways = jnp.concatenate(
            [gradient * powers[rows, 0:128], gradient * powers[rows, 128:256]], axis=1
        )
        pick = (pick_row == pick_half + block).astype(BF16)
        for index, part in enumerate(split3(both_ways)):
            parts[index, rows] = part
            ends = ends + lax.dot_general(
                pick, part, (((1,), (1,)), ((), ())), preferred_element_type=F32
            )

    xbuf[0] = ends
    x_copies = [
        remote(xbuf.at[0], xbuf.at[step], xs.at[step - 1], xr.at[step - 1], x_peer(step), lat)
        for step in range(1, XG)
    ]
    for copy in x_copies:
        copy.start()

    def local_sums(block, carry):
        col = iota((256, 256), 1)
        row = iota((256, 256), 0)
        ahead = ((row < 128) & (col < 128) & (row <= col)) | (
            (row >= 128) & (col >= 128) & (row > col)
        )
        ahead = ahead.astype(F32).astype(BF16)
        rows = pl.ds(pl.multiple_of(block * 128, 128), 128)
        total = jnp.dot(parts[0, rows], ahead, preferred_element_type=F32)
        total = total + jnp.dot(parts[1, rows], ahead, preferred_element_type=F32)
        total = total + jnp.dot(parts[2, rows], ahead, preferred_element_type=F32)
        sums[rows] = total
        return carry

    forward_half = sub8 < 4
    for copy in x_copies:
        copy.wait_recv()
    group = jnp.zeros((8, 128), F32)
    inside = jnp.zeros((8, 128), F32)
    for step in range(XG):
        source = lax.rem(x_pos + XG - step, XG)
        tile = xbuf[step]
        to_end = jnp.where(forward_half, XG - 1 - source, source).astype(F32)
        group = group + jnp.exp(log_block * to_end) * tile
        ahead = jnp.where(forward_half, x_pos - source, source - x_pos)
        reach = jnp.exp(log_block * jnp.maximum(ahead - 1, 0).astype(F32))
        inside = inside + jnp.where(ahead > 0, reach * tile, 0.0)
    zbuf[0] = group
    z_copies = [
        remote(zbuf.at[0], zbuf.at[step], zs.at[step - 1], zr.at[step - 1], z_peer(step), lat)
        for step in range(1, nz)
    ]
    for copy in z_copies:
        copy.start()

    lax.fori_loop(0, 4, local_sums, 0)

    for copy in z_copies:
        copy.wait_recv()
    inflow = zbuf[0]
    for step in range(nz - 1, 0, -1):
        inflow = inflow * group_decay + jnp.where(forward_half, zbuf[step], zbuf[nz - step])
    steps_in = jnp.where(forward_half, x_pos, XG - 1 - x_pos).astype(F32)
    inflow = inside + jnp.exp(log_block * steps_in) * (inflow / image_sum)
    inflow = inflow * block_decay
    inflow_cols = jnp.concatenate([inflow] * 16, axis=0).T
    for block in range(4):
        rows = pl.ds(block * 128, 128)
        east_in = jnp.broadcast_to(inflow_cols[:, block : block + 1], (128, 128))
        west_in = jnp.broadcast_to(inflow_cols[:, block + 4 : block + 5], (128, 128))
        grad_buf[rows] = gains[rows, 0:128] * (sums[rows, 0:128] + east_in) + gains[
            rows, 128:256
        ] * (sums[rows, 128:256] + west_in)
    grad_out = pltpu.make_async_copy(grad_buf, grad_hbm, out_sem.at[1])
    grad_out.start()

    to_west.wait_send()
    to_east.wait_send()

    @pl.when(top)
    def _():
        @pl.when(jnp.logical_not(nw_self))
        def _():
            fold_to_nw.wait_send()

        @pl.when(jnp.logical_not(ne_self))
        def _():
            fold_to_ne.wait_send()

    @pl.when(jnp.logical_not(top))
    def _():
        to_nw.wait_send()
        to_ne.wait_send()

    @pl.when(jnp.logical_not(low))
    def _():
        to_sw.wait_send()
        to_se.wait_send()

    for copy in x_copies:
        copy.wait_send()
    for copy in z_copies:
        copy.wait_send()
    eta_out.wait()
    grad_out.wait()


def local(
    wet_mask, east_level, north_level, courant, increment, innovation, obs_weight, smooth_scale
):
    nlon = lax.axis_size("lon")
    nlat = lax.axis_size("lat")
    nz = nlon // XG
    any_space = pl.BlockSpec(memory_space=pl.ANY)
    dma = pltpu.SemaphoreType.DMA
    block = jax.ShapeDtypeStruct((512, 128), F32)
    return pl.pallas_call(
        functools.partial(kernel, nlon, nlat),
        out_shape=(block, block),
        in_specs=[any_space] * 7 + [pl.BlockSpec(memory_space=pltpu.VMEM)],
        out_specs=(any_space, any_space),
        scratch_shapes=[
            pltpu.VMEM((3, 512, 128), jnp.int32),
            pltpu.VMEM((2, 512, 128), F32),
            pltpu.VMEM((FIELDS, 544, 128), F32),
            pltpu.VMEM((FIELDS, 544, 128), F32),
            pltpu.VMEM((2, 544, 128), F32),
            pltpu.VMEM((2, 544, 128), F32),
            pltpu.VMEM((512, 128), F32),
            pltpu.VMEM((8, 2, 8, 512), F32),
            pltpu.VMEM((8, 2, 8, 512), F32),
            pltpu.VMEM((4, 8, 128), F32),
            pltpu.VMEM((512, 128), F32),
            pltpu.VMEM((512, 128), F32),
            pltpu.VMEM((512, 256), F32),
            pltpu.VMEM((512, 256), F32),
            pltpu.VMEM((3, 512, 256), BF16),
            pltpu.VMEM((512, 256), F32),
            pltpu.VMEM((XG, 8, 128), F32),
            pltpu.VMEM((nz, 8, 128), F32),
            dma((7,)),
            dma((2,)),
            dma((8,)),
            dma((8,)),
            dma((XG - 1,)),
            dma((XG - 1,)),
            dma((nz - 1,)),
            dma((nz - 1,)),
        ],
        compiler_params=pltpu.CompilerParams(
            collective_id=0, has_side_effects=True, vmem_limit_bytes=32 * 1024 * 1024
        ),
    )(
        wet_mask,
        east_level,
        north_level,
        courant,
        increment,
        innovation,
        obs_weight,
        smooth_scale.reshape(4, 128),
    )


def solution(mesh):
    return jax.shard_map(
        local,
        mesh=mesh,
        in_specs=(P("lat", "lon"),) * 7 + (P("lat"),),
        out_specs=(P("lat", "lon"), P("lat", "lon")),
        check_vma=False,
    )
```

```python
import functools
import jax
import jax.numpy as jnp
from jax import lax
from jax.experimental import pallas as pl
from jax.experimental.pallas import tpu as pltpu
from jax.sharding import PartitionSpec as P

SUBSTEPS = 4
WLEV = 8
F32 = jnp.float32
BF16 = jnp.bfloat16
XG = 4
FIELDS = 6
WEST = 6
PAD = 16
RH = 24
HIGH = lax.Precision.HIGHEST


def roll(value, shift, axis):
    return pltpu.roll(value, shift % value.shape[axis], axis)


def iota(shape, dim):
    return lax.broadcasted_iota(jnp.int32, shape, dim)


def split3(value):
    high = value.astype(BF16)
    rest = value - high.astype(F32)
    mid = rest.astype(BF16)
    low = (rest - mid.astype(F32)).astype(BF16)
    return high, mid, low


def remote(src, dst, send_sem, recv_sem, lon, lat):
    return pltpu.make_async_remote_copy(
        src_ref=src,
        dst_ref=dst,
        send_sem=send_sem,
        recv_sem=recv_sem,
        device_id={"lon": lon, "lat": lat},
        device_id_type=pl.DeviceIdType.MESH,
    )


def kernel(
    nlon,
    nlat,
    wet_hbm,
    east_hbm,
    north_hbm,
    cour_hbm,
    incr_hbm,
    innov_hbm,
    ow_hbm,
    scale_hbm,
    eta_ref,
    grad_ref,
    raw_i,
    raw_f,
    main,
    halo,
    work,
    delta,
    packed,
    strip_out,
    strip_in,
    corner,
    scale_buf,
    powers,
    gains,
    parts,
    sums,
    xbuf,
    zbuf,
    in_sem,
    hs,
    hr,
    xs,
    xr,
    zs,
    zr,
):
    lon = lax.axis_index("lon")
    lat = lax.axis_index("lat")
    nz = nlon // XG
    x_pos = lax.rem(lon, XG)
    z_pos = lon // XG
    top = lat == nlat - 1
    low = lat == 0
    east_lon = lax.rem(lon + 1, nlon)
    west_lon = lax.rem(lon + nlon - 1, nlon)
    fold_lon = nlon - 1 - lon
    fold_ne = lax.rem(2 * nlon - 2 - lon, nlon)
    fold_nw = lax.rem(nlon - lon, nlon)
    ne_self = fold_ne == lon
    nw_self = fold_nw == lon

    loads = [
        pltpu.make_async_copy(scale_hbm, scale_buf, in_sem.at[7]),
        pltpu.make_async_copy(wet_hbm, raw_i.at[0], in_sem.at[0]),
        pltpu.make_async_copy(cour_hbm, raw_f.at[0], in_sem.at[1]),
        pltpu.make_async_copy(incr_hbm, raw_f.at[1], in_sem.at[2]),
        pltpu.make_async_copy(east_hbm, raw_i.at[1], in_sem.at[3]),
        pltpu.make_async_copy(north_hbm, raw_i.at[2], in_sem.at[4]),
        pltpu.make_async_copy(ow_hbm, main.at[4, pl.ds(PAD, 512)], in_sem.at[5]),
        pltpu.make_async_copy(innov_hbm, main.at[5, pl.ds(PAD, 512)], in_sem.at[6]),
    ]
    for load in loads:
        load.start()

    barrier = pltpu.get_barrier_semaphore()

    def greet(to_lon, to_lat):
        pl.semaphore_signal(
            barrier,
            inc=1,
            device_id={"lon": to_lon, "lat": to_lat},
            device_id_type=pl.DeviceIdType.MESH,
        )

    def x_peer(step):
        return z_pos * XG + lax.rem(x_pos + step, XG)

    def z_peer(step):
        return lax.rem(z_pos + step, nz) * XG + x_pos

    greet(east_lon, lat)
    greet(west_lon, lat)

    @pl.when(jnp.logical_not(low))
    def _():
        greet(lon, lat - 1)
        greet(east_lon, lat - 1)
        greet(west_lon, lat - 1)

    @pl.when(jnp.logical_not(top))
    def _():
        greet(lon, lat + 1)
        greet(east_lon, lat + 1)
        greet(west_lon, lat + 1)

    @pl.when(top)
    def _():
        greet(fold_lon, lat)

        @pl.when(jnp.logical_not(ne_self))
        def _():
            greet(fold_ne, lat)

        @pl.when(jnp.logical_not(nw_self))
        def _():
            greet(fold_nw, lat)

    for step in range(1, XG):
        greet(x_peer(step), lat)
    for step in range(1, nz):
        greet(z_peer(step), lat)

    lane8 = iota((8, 128), 1)
    sub8 = iota((8, 128), 0)

    zero8 = jnp.zeros((8, 128), F32)
    zstrip = jnp.zeros((8, 512), F32)
    strip_in[0, 0] = zstrip
    strip_in[6, 1] = zstrip
    strip_in[7, 0] = zstrip
    strip_in[7, 1] = zstrip
    for edge in (0, 536):
        for field in (0, 3):
            main[field, pl.ds(edge, 8)] = zero8
            halo[field, pl.ds(edge, 8)] = zero8
        work[0, pl.ds(edge, 8)] = zero8
        work[1, pl.ds(edge, 8)] = zero8

    @pl.when(low)
    def _():
        for field in range(FIELDS):
            main[field, pl.ds(8, 8)] = zero8
        corner[0] = zero8
        corner[1] = zero8

    for load in loads:
        load.wait()
    slot = (iota((32, 128), 1) + 8) // 16
    for block in range(4):
        for row in range(128 * block, 128 * block + 128, 32):
            rows, own = pl.ds(row, 32), pl.ds(row + PAD, 32)
            wet = raw_i[0, rows].astype(F32)
            fields = [
                wet * raw_f[1, rows],
                wet * raw_f[0, rows],
                raw_i[1, rows].astype(F32) * (1.0 / WLEV),
                raw_i[2, rows].astype(F32) * (1.0 / WLEV),
            ]
            for index, value in enumerate(fields):
                main[index, own] = value
            main[WEST, own] = roll(fields[2], 1, 1)
            fields.append(main[4, own])
            fields.append(main[5, own])
            joined = roll(fields[0], 16, 1)
            for index in range(1, FIELDS):
                moved = roll(fields[index], 16 * (index + 1), 1)
                joined = jnp.where(slot == index + 1, moved, joined)
            packed[rows] = joined
        rows = pl.ds(128 * block, 128)
        strip_out[:, :, :, rows] = packed[rows].T.reshape(8, 2, 8, 128)

    links = 2 + (XG - 1) + (nz - 1)
    north_links = jnp.where(
        top, 3 - ne_self.astype(jnp.int32) - nw_self.astype(jnp.int32), 3
    )
    south_links = jnp.where(low, 0, 3)
    pl.semaphore_wait(barrier, links + north_links + south_links)

    top_rows = main.at[pl.ds(0, FIELDS), pl.ds(PAD + 504, 8)]
    low_rows = main.at[pl.ds(0, FIELDS), pl.ds(PAD, 8)]
    south_halo = main.at[pl.ds(0, FIELDS), pl.ds(8, 8)]
    north_halo = main.at[pl.ds(0, FIELDS), pl.ds(PAD + 512, 8)]
    top_tile = packed.at[pl.ds(504, 8)]
    low_tile = packed.at[pl.ds(0, 8)]
    to_west = remote(
        strip_out.at[pl.ds(1, 6), 0], strip_in.at[pl.ds(1, 6), 0], hs.at[2], hr.at[3], west_lon, lat
    )
    to_east = remote(
        strip_out.at[pl.ds(0, 6), 1], strip_in.at[pl.ds(0, 6), 1], hs.at[3], hr.at[2], east_lon, lat
    )
    to_south = remote(low_rows, north_halo, hs.at[0], hr.at[1], lon, lat - 1)
    to_sw = remote(low_tile, corner.at[3], hs.at[4], hr.at[7], west_lon, lat - 1)
    to_se = remote(low_tile, corner.at[2], hs.at[5], hr.at[6], east_lon, lat - 1)
    to_north = remote(top_rows, south_halo, hs.at[1], hr.at[0], lon, lat + 1)
    to_nw = remote(top_tile, corner.at[1], hs.at[6], hr.at[5], west_lon, lat + 1)
    to_ne = remote(top_tile, corner.at[0], hs.at[7], hr.at[4], east_lon, lat + 1)
    over_fold = remote(top_rows, north_halo, hs.at[1], hr.at[1], fold_lon, lat)
    fold_to_nw = remote(top_tile, corner.at[2], hs.at[6], hr.at[6], fold_nw, lat)
    fold_to_ne = remote(top_tile, corner.at[3], hs.at[7], hr.at[7], fold_ne, lat)
    own_nw = pltpu.make_async_copy(top_tile, corner.at[2], hr.at[6])
    own_ne = pltpu.make_async_copy(top_tile, corner.at[3], hr.at[7])

    to_west.start()
    to_east.start()

    @pl.when(top)
    def _():
        over_fold.start()

        @pl.when(jnp.logical_not(nw_self))
        def _():
            fold_to_nw.start()

        @pl.when(nw_self)
        def _():
            own_nw.start()

        @pl.when(jnp.logical_not(ne_self))
        def _():
            fold_to_ne.start()

        @pl.when(ne_self)
        def _():
            own_ne.start()

    @pl.when(jnp.logical_not(top))
    def _():
        to_north.start()
        to_nw.start()
        to_ne.start()

    @pl.when(jnp.logical_not(low))
    def _():
        to_south.start()
        to_sw.start()
        to_se.start()

    scale = scale_buf[...]
    scale = jnp.concatenate([scale, scale], axis=0)
    stiff = scale * float(128 * 128)
    root_term = jnp.sqrt(1.0 + 4.0 * stiff)
    log_root = jnp.log1p(-(root_term - 1.0) / (2.0 * stiff))
    gain = (1.0 / root_term) * (2.0 * jnp.sqrt(jnp.sqrt(stiff)))
    both = jnp.where(sub8 < 4, log_root, gain)
    columns = jnp.concatenate([both] * 16, axis=0).T
    place = iota((128, 128), 1).astype(F32) - 63.5
    for block in range(4):
        rows = pl.ds(block * 128, 128)
        power = jnp.broadcast_to(columns[:, block : block + 1], (128, 128)) * place
        gain_rows = jnp.broadcast_to(columns[:, block + 4 : block + 5], (128, 128))
        up = jnp.exp(power)
        down = jnp.exp(-power)
        powers[rows, 0:128] = down
        powers[rows, 128:256] = up
        gains[rows, 0:128] = gain_rows * up
        gains[rows, 128:256] = gain_rows * down
    log_block = log_root * 128.0
    block_decay = jnp.exp(log_block)
    group_decay = jnp.exp(log_block * float(XG))
    image_sum = 1.0 - jnp.exp(log_block * float(nlon))

    for row in range(8, 536, RH):
        delta[0, pl.ds(row, RH)] = jnp.zeros((RH, 128), F32)
        delta[1, pl.ds(row, RH)] = jnp.zeros((RH, 128), F32)

    first_half = lax.rem(lane8, 16) < 8
    to_east.wait_recv()
    to_west.wait_recv()

    def set_west(rows, outer):
        inner = main[WEST, rows]
        first = iota(inner.shape, 1) == 0
        main[WEST, rows] = jnp.where(first, outer, inner)
        halo[WEST, rows] = jnp.where(first, inner, outer)

    for block in range(4):
        own = pl.ds(128 * block + PAD, 128)
        edges = strip_in[:, :, :, pl.ds(128 * block, 128)].reshape(128, 128).T
        for field in range(FIELDS):
            halo[field, own] = roll(edges, -16 * (field + 1), 1)
        set_west(own, roll(edges, 1 - 16 * 3, 1))

    @pl.when(jnp.logical_not(low))
    def _():
        to_north.wait_recv()
        to_nw.wait_recv()
        to_ne.wait_recv()

    south_corner = jnp.where(first_half, corner[1], corner[0])
    for field in range(FIELDS):
        halo[field, pl.ds(8, 8)] = roll(south_corner, -16 * (field + 1), 1)
    to_south.wait_recv()
    to_sw.wait_recv()
    to_se.wait_recv()

    @pl.when(top)
    def _():
        over_fold.wait_send()

    @pl.when(jnp.logical_not(top))
    def _():
        to_north.wait_send()

    @pl.when(jnp.logical_not(low))
    def _():
        to_south.wait_send()

    @pl.when(jnp.logical_not(top))
    def _():
        north_corner = jnp.where(first_half, corner[3], corner[2])
        for field in range(FIELDS):
            halo[field, pl.ds(PAD + 512, 8)] = roll(north_corner, -16 * (field + 1), 1)

    @pl.when(top)
    def _():
        mixed = jnp.where(first_half, corner[2], corner[3])
        tiles = [main[field, pl.ds(PAD + 512, 8)] for field in range(FIELDS)] + [mixed, zero8]
        stack = jnp.concatenate(tiles, axis=0)
        flip = (iota((128, 128), 0) + iota((128, 128), 1) == 127).astype(F32)
        row_to = iota((64, 64), 0)
        row_from = iota((64, 64), 1)
        swap = (row_to // 8 == row_from // 8) & (row_to % 8 + row_from % 8 == 7)
        turned = jnp.dot(stack, flip, precision=HIGH, preferred_element_type=F32)
        turned = jnp.dot(swap.astype(F32), turned, precision=HIGH, preferred_element_type=F32)
        ghost = pl.ds(PAD + 512, 8)
        for field in range(FIELDS):
            inner = turned[8 * field : 8 * field + 8]
            outer = roll(turned[48:56], 16 * (field + 1), 1)
            if field == 2:
                inner, outer = roll(inner, -1, 1), roll(outer, -1, 1)
                inner, outer = (
                    jnp.where(lane8 == 127, outer, inner),
                    jnp.where(lane8 == 127, inner, outer),
                )
            if field == 3:
                last = pl.ds(PAD + 504, 8)
                main[3, last] = jnp.where(sub8 == 7, main[3, last] * inner[0:1], main[3, last])
                halo[3, last] = jnp.where(sub8 == 7, halo[3, last] * outer[0:1], halo[3, last])
                inner, outer = roll(inner, -1, 0), roll(outer, -1, 0)
            main[field, ghost] = inner
            halo[field, ghost] = outer

    for edge in (8, PAD + 512):
        rows = pl.ds(edge, 8)
        main[WEST, rows] = roll(main[2, rows], 1, 1)
        set_west(rows, roll(halo[2, rows], 1, 1))

    last_lane = iota((RH, 128), 1) == 127
    zero_lane = iota((RH, 128), 1) == 0

    def substep(src, dst):
        for row in range(8, 536, RH):
            here, up, down = pl.ds(row, RH), pl.ds(row + 1, RH), pl.ds(row - 1, RH)
            states = [src[side][here] for side in range(2)]
            east = [roll(state, -1, 1) for state in states]
            west = [roll(state, 1, 1) for state in states]
            for side, field in enumerate((main, halo)):
                state = states[side]
                to_east = jnp.where(last_lane, east[1 - side], east[side]) - state
                to_west = jnp.where(zero_lane, west[1 - side], west[side]) - state
                spread = field[2, here] * to_east + field[WEST, here] * to_west
                spread = spread + field[3, here] * (src[side][up] - state)
                spread = spread + field[3, down] * (src[side][down] - state)
                change = delta[side, here] + field[1, here] * spread
                delta[side, here] = change
                dst[side][here] = state + change

    side_a = (main.at[0], halo.at[0])
    side_b = (work.at[0], work.at[1])

    def forward_pair(step, carry):
        substep(side_a, side_b)
        substep(side_b, side_a)
        return carry

    lax.fori_loop(0, SUBSTEPS // 2, forward_pair, 0)

    for row in range(8, 536, RH):
        here = pl.ds(row, RH)
        for side, field in enumerate((main, halo)):
            start = field[1, here] * field[4, here] * (field[0, here] - field[5, here])
            work[side, here] = start
            delta[side, here] = start
    eta_ref[...] = main[0, pl.ds(PAD, 512)]

    def adjoint_pair(step, carry):
        substep(side_b, side_a)
        substep(side_a, side_b)
        return carry

    lax.fori_loop(0, SUBSTEPS // 2, adjoint_pair, 0)

    ends = jnp.zeros((8, 128), F32)
    pick_row = iota((8, 256), 0)
    pick_half = 4 * (iota((8, 256), 1) // 128)
    for block in range(4):
        rows = pl.ds(block * 128, 128)
        gradient = delta[0, pl.ds(PAD + block * 128, 128)] / raw_f[0, rows]
        both_ways = jnp.concatenate(
            [gradient * powers[rows, 0:128], gradient * powers[rows, 128:256]], axis=1
        )
        pick = (pick_row == pick_half + block).astype(BF16)
        for index, part in enumerate(split3(both_ways)):
            parts[index, rows] = part
            ends = ends + lax.dot_general(
                pick, part, (((1,), (1,)), ((), ())), preferred_element_type=F32
            )

    xbuf[0] = ends
    x_copies = [
        remote(xbuf.at[0], xbuf.at[step], xs.at[step - 1], xr.at[step - 1], x_peer(step), lat)
        for step in (2, 1, 3)
    ]
    for copy in x_copies:
        copy.start()

    forward_half = sub8 < 4
    for copy in x_copies:
        copy.wait_recv()
    group = jnp.zeros((8, 128), F32)
    inside = jnp.zeros((8, 128), F32)
    for step in range(XG):
        source = lax.rem(x_pos + XG - step, XG)
        tile = xbuf[step]
        to_end = jnp.where(forward_half, XG - 1 - source, source).astype(F32)
        group = group + jnp.exp(log_block * to_end) * tile
        ahead = jnp.where(forward_half, x_pos - source, source - x_pos)
        reach = jnp.exp(log_block * jnp.maximum(ahead - 1, 0).astype(F32))
        inside = inside + jnp.where(ahead > 0, reach * tile, 0.0)
    zbuf[0] = group
    z_copies = [
        remote(zbuf.at[0], zbuf.at[step], zs.at[step - 1], zr.at[step - 1], z_peer(step), lat)
        for step in sorted(range(1, nz), key=lambda step: -min(step, nz - step))
    ]
    for copy in z_copies:
        copy.start()

    col = iota((256, 256), 1)
    row = iota((256, 256), 0)
    ahead = ((row < 128) & (col < 128) & (row <= col)) | ((row >= 128) & (col >= 128) & (row > col))
    ahead = ahead.astype(F32).astype(BF16)
    for block in range(4):
        rows = pl.ds(block * 128, 128)
        total = jnp.dot(parts[0, rows], ahead, preferred_element_type=F32)
        total = total + jnp.dot(parts[1, rows], ahead, preferred_element_type=F32)
        sums[rows] = total + jnp.dot(parts[2, rows], ahead, preferred_element_type=F32)

    for copy in z_copies:
        copy.wait_recv()
    inflow = zbuf[0]
    for step in range(nz - 1, 0, -1):
        inflow = inflow * group_decay + jnp.where(forward_half, zbuf[step], zbuf[nz - step])
    steps_in = jnp.where(forward_half, x_pos, XG - 1 - x_pos).astype(F32)
    inflow = inside + jnp.exp(log_block * steps_in) * (inflow / image_sum)
    inflow = inflow * block_decay
    inflow_cols = jnp.concatenate([inflow] * 16, axis=0).T
    for block in range(4):
        rows = pl.ds(block * 128, 128)
        east_in = jnp.broadcast_to(inflow_cols[:, block : block + 1], (128, 128))
        west_in = jnp.broadcast_to(inflow_cols[:, block + 4 : block + 5], (128, 128))
        grad_ref[rows] = gains[rows, 0:128] * (sums[rows, 0:128] + east_in) + gains[
            rows, 128:256
        ] * (sums[rows, 128:256] + west_in)

    to_west.wait_send()
    to_east.wait_send()

    @pl.when(top)
    def _():
        @pl.when(jnp.logical_not(nw_self))
        def _():
            fold_to_nw.wait_send()

        @pl.when(jnp.logical_not(ne_self))
        def _():
            fold_to_ne.wait_send()

    @pl.when(jnp.logical_not(top))
    def _():
        to_nw.wait_send()
        to_ne.wait_send()

    @pl.when(jnp.logical_not(low))
    def _():
        to_sw.wait_send()
        to_se.wait_send()

    for copy in x_copies:
        copy.wait_send()
    for copy in z_copies:
        copy.wait_send()


def local(
    wet_mask, east_level, north_level, courant, increment, innovation, obs_weight, smooth_scale
):
    nlon = lax.axis_size("lon")
    nlat = lax.axis_size("lat")
    nz = nlon // XG
    hbm = pl.BlockSpec(memory_space=pltpu.MemorySpace.HBM)
    vmem = pl.BlockSpec(memory_space=pltpu.VMEM)
    dma = pltpu.SemaphoreType.DMA
    block = jax.ShapeDtypeStruct((512, 128), F32)
    return pl.pallas_call(
        functools.partial(kernel, nlon, nlat),
        out_shape=(block, block),
        in_specs=[hbm] * 8,
        out_specs=(vmem, vmem),
        scratch_shapes=[
            pltpu.VMEM((3, 512, 128), jnp.int32),
            pltpu.VMEM((2, 512, 128), F32),
            pltpu.VMEM((FIELDS + 1, 544, 128), F32),
            pltpu.VMEM((FIELDS + 1, 544, 128), F32),
            pltpu.VMEM((2, 544, 128), F32),
            pltpu.VMEM((2, 544, 128), F32),
            pltpu.VMEM((512, 128), F32),
            pltpu.VMEM((8, 2, 8, 512), F32),
            pltpu.VMEM((8, 2, 8, 512), F32),
            pltpu.VMEM((4, 8, 128), F32),
            pltpu.VMEM((4, 128), F32),
            pltpu.VMEM((512, 256), F32),
            pltpu.VMEM((512, 256), F32),
            pltpu.VMEM((3, 512, 256), BF16),
            pltpu.VMEM((512, 256), F32),
            pltpu.VMEM((XG, 8, 128), F32),
            pltpu.VMEM((nz, 8, 128), F32),
            dma((8,)),
            dma((8,)),
            dma((8,)),
            dma((XG - 1,)),
            dma((XG - 1,)),
            dma((nz - 1,)),
            dma((nz - 1,)),
        ],
        compiler_params=pltpu.CompilerParams(
            collective_id=0, has_side_effects=True, vmem_limit_bytes=54656 * 1024
        ),
    )(
        wet_mask,
        east_level,
        north_level,
        courant,
        increment,
        innovation,
        obs_weight,
        smooth_scale.reshape(4, 128),
    )


def solution(mesh):
    return jax.shard_map(
        local,
        mesh=mesh,
        in_specs=(P("lat", "lon"),) * 7 + (P("lat"),),
        out_specs=(P("lat", "lon"), P("lat", "lon")),
        check_vma=False,
    )
```

```python
import functools
import jax
import jax.numpy as jnp
from jax import lax
from jax.experimental import pallas as pl
from jax.experimental.pallas import tpu as pltpu
from jax.sharding import PartitionSpec as P

SUBSTEPS = 4
WLEV = 8
F32 = jnp.float32
BF16 = jnp.bfloat16
XG = 4
FIELDS = 6
WEST = 6
PAD = 16
RH = 24
HIGH = lax.Precision.HIGHEST


def roll(value, shift, axis):
    return pltpu.roll(value, shift % value.shape[axis], axis)


def iota(shape, dim):
    return lax.broadcasted_iota(jnp.int32, shape, dim)


def split3(value):
    high = value.astype(BF16)
    rest = value - high.astype(F32)
    mid = rest.astype(BF16)
    low = (rest - mid.astype(F32)).astype(BF16)
    return high, mid, low


def remote(src, dst, send_sem, recv_sem, lon, lat):
    return pltpu.make_async_remote_copy(
        src_ref=src,
        dst_ref=dst,
        send_sem=send_sem,
        recv_sem=recv_sem,
        device_id={"lon": lon, "lat": lat},
        device_id_type=pl.DeviceIdType.MESH,
    )


def kernel(
    nlon,
    nlat,
    wet_hbm,
    east_hbm,
    north_hbm,
    cour_hbm,
    incr_hbm,
    innov_hbm,
    ow_hbm,
    scale_hbm,
    eta_ref,
    grad_ref,
    raw_i,
    raw_f,
    main,
    halo,
    work,
    delta,
    packed,
    strip_out,
    strip_in,
    corner,
    scale_buf,
    powers,
    gains,
    parts,
    sums,
    xbuf,
    zbuf,
    z_weight,
    in_sem,
    hs,
    hr,
    xs,
    xr,
    zs,
    zr,
):
    lon = lax.axis_index("lon")
    lat = lax.axis_index("lat")
    nz = nlon // XG
    x_pos = lax.rem(lon, XG)
    z_pos = lon // XG
    top = lat == nlat - 1
    low = lat == 0
    east_lon = lax.rem(lon + 1, nlon)
    west_lon = lax.rem(lon + nlon - 1, nlon)
    fold_lon = nlon - 1 - lon
    fold_ne = lax.rem(2 * nlon - 2 - lon, nlon)
    fold_nw = lax.rem(nlon - lon, nlon)
    ne_self = fold_ne == lon
    nw_self = fold_nw == lon

    loads = [
        pltpu.make_async_copy(scale_hbm, scale_buf, in_sem.at[7]),
        pltpu.make_async_copy(wet_hbm, raw_i.at[0], in_sem.at[0]),
        pltpu.make_async_copy(cour_hbm, raw_f.at[0], in_sem.at[1]),
        pltpu.make_async_copy(incr_hbm, raw_f.at[1], in_sem.at[2]),
        pltpu.make_async_copy(east_hbm, raw_i.at[1], in_sem.at[3]),
        pltpu.make_async_copy(north_hbm, raw_i.at[2], in_sem.at[4]),
        pltpu.make_async_copy(ow_hbm, main.at[4, pl.ds(PAD, 512)], in_sem.at[5]),
        pltpu.make_async_copy(innov_hbm, main.at[5, pl.ds(PAD, 512)], in_sem.at[6]),
    ]
    barrier = pltpu.get_barrier_semaphore()

    def greet(to_lon, to_lat):
        pl.semaphore_signal(
            barrier,
            inc=1,
            device_id={"lon": to_lon, "lat": to_lat},
            device_id_type=pl.DeviceIdType.MESH,
        )

    def x_peer(step):
        return z_pos * XG + lax.rem(x_pos + step, XG)

    def z_peer(step):
        return lax.rem(z_pos + step, nz) * XG + x_pos

    greet(east_lon, lat)
    greet(west_lon, lat)

    @pl.when(jnp.logical_not(low))
    def _():
        greet(lon, lat - 1)
        greet(east_lon, lat - 1)
        greet(west_lon, lat - 1)

    @pl.when(jnp.logical_not(top))
    def _():
        greet(lon, lat + 1)
        greet(east_lon, lat + 1)
        greet(west_lon, lat + 1)

    @pl.when(top)
    def _():
        greet(fold_lon, lat)

        @pl.when(jnp.logical_not(ne_self))
        def _():
            greet(fold_ne, lat)

        @pl.when(jnp.logical_not(nw_self))
        def _():
            greet(fold_nw, lat)

    for load in loads:
        load.start()
    far_first = sorted(range(1, nz), key=lambda step: -min(step, nz - step))
    for step in far_first:
        greet(z_peer(step), lat)
    for step in range(1, XG):
        greet(x_peer(step), lat)

    lane8 = iota((8, 128), 1)
    sub8 = iota((8, 128), 0)

    zero8 = jnp.zeros((8, 128), F32)
    for block in range(4):
        for slot, side in ((0, 0), (6, 1), (7, 0), (7, 1)):
            strip_in[block, slot, side] = zero8
    for edge in (0, 536):
        for field in (0, 3):
            main[field, pl.ds(edge, 8)] = zero8
            halo[field, pl.ds(edge, 8)] = zero8
        work[0, pl.ds(edge, 8)] = zero8
        work[1, pl.ds(edge, 8)] = zero8

    @pl.when(low)
    def _():
        for field in range(FIELDS):
            main[field, pl.ds(8, 8)] = zero8
        corner[0] = zero8
        corner[1] = zero8

    for load in loads:
        load.wait()
    slot = (iota((32, 128), 1) + 8) // 16
    for block in range(4):
        for row in range(128 * block, 128 * block + 128, 32):
            rows, own = pl.ds(row, 32), pl.ds(row + PAD, 32)
            wet = raw_i[0, rows].astype(F32)
            fields = [
                wet * raw_f[1, rows],
                wet * raw_f[0, rows],
                raw_i[1, rows].astype(F32) * (1.0 / WLEV),
                raw_i[2, rows].astype(F32) * (1.0 / WLEV),
            ]
            for index, value in enumerate(fields):
                main[index, own] = value
            main[WEST, own] = roll(fields[2], 1, 1)
            fields.append(main[4, own])
            fields.append(main[5, own])
            joined = roll(fields[0], 16, 1)
            for index in range(1, FIELDS):
                moved = roll(fields[index], 16 * (index + 1), 1)
                joined = jnp.where(slot == index + 1, moved, joined)
            packed[rows] = joined

    links = 2 + (XG - 1) + (nz - 1)
    north_links = jnp.where(
        top, 3 - ne_self.astype(jnp.int32) - nw_self.astype(jnp.int32), 3
    )
    south_links = jnp.where(low, 0, 3)
    pl.semaphore_wait(barrier, links + north_links + south_links)

    top_rows = main.at[pl.ds(0, FIELDS), pl.ds(PAD + 504, 8)]
    low_rows = main.at[pl.ds(0, FIELDS), pl.ds(PAD, 8)]
    south_halo = main.at[pl.ds(0, FIELDS), pl.ds(8, 8)]
    north_halo = main.at[pl.ds(0, FIELDS), pl.ds(PAD + 512, 8)]
    top_tile = packed.at[pl.ds(504, 8)]
    low_tile = packed.at[pl.ds(0, 8)]
    to_west, to_east = [], []
    for block in range(4):
        first = strip_out.at[block, pl.ds(1, 6), 0], strip_in.at[block, pl.ds(1, 6), 0]
        last = strip_out.at[block, pl.ds(0, 6), 1], strip_in.at[block, pl.ds(0, 6), 1]
        to_west.append(remote(*first, hs.at[8 + block], hr.at[8 + block], west_lon, lat))
        to_east.append(remote(*last, hs.at[12 + block], hr.at[12 + block], east_lon, lat))
    to_south = remote(low_rows, north_halo, hs.at[0], hr.at[1], lon, lat - 1)
    to_sw = remote(low_tile, corner.at[3], hs.at[4], hr.at[7], west_lon, lat - 1)
    to_se = remote(low_tile, corner.at[2], hs.at[5], hr.at[6], east_lon, lat - 1)
    to_north = remote(top_rows, south_halo, hs.at[1], hr.at[0], lon, lat + 1)
    to_nw = remote(top_tile, corner.at[1], hs.at[6], hr.at[5], west_lon, lat + 1)
    to_ne = remote(top_tile, corner.at[0], hs.at[7], hr.at[4], east_lon, lat + 1)
    over_fold = remote(top_rows, north_halo, hs.at[1], hr.at[1], fold_lon, lat)
    fold_to_nw = remote(top_tile, corner.at[2], hs.at[6], hr.at[6], fold_nw, lat)
    fold_to_ne = remote(top_tile, corner.at[3], hs.at[7], hr.at[7], fold_ne, lat)
    own_nw = pltpu.make_async_copy(top_tile, corner.at[2], hr.at[6])
    own_ne = pltpu.make_async_copy(top_tile, corner.at[3], hr.at[7])

    @pl.when(top)
    def _():
        over_fold.start()

        @pl.when(jnp.logical_not(nw_self))
        def _():
            fold_to_nw.start()

        @pl.when(nw_self)
        def _():
            own_nw.start()

        @pl.when(jnp.logical_not(ne_self))
        def _():
            fold_to_ne.start()

        @pl.when(ne_self)
        def _():
            own_ne.start()

    @pl.when(jnp.logical_not(top))
    def _():
        to_north.start()
        to_nw.start()
        to_ne.start()

    @pl.when(jnp.logical_not(low))
    def _():
        to_south.start()
        to_sw.start()
        to_se.start()

    for block in range(4):
        turned = packed[pl.ds(128 * block, 128)].T
        strip_out[block] = turned.reshape(8, 2, 8, 128)
        to_west[block].start()
        to_east[block].start()

    scale = scale_buf[...]
    scale = jnp.concatenate([scale, scale], axis=0)
    stiff = scale * float(128 * 128)
    root_term = jnp.sqrt(1.0 + 4.0 * stiff)
    log_root = jnp.log1p(-(root_term - 1.0) / (2.0 * stiff))
    gain = (1.0 / root_term) * (2.0 * jnp.sqrt(jnp.sqrt(stiff)))
    both = jnp.where(sub8 < 4, log_root, gain)
    columns = jnp.concatenate([both] * 16, axis=0).T
    place = iota((128, 128), 1).astype(F32) - 63.5
    for block in range(4):
        rows = pl.ds(block * 128, 128)
        power = jnp.broadcast_to(columns[:, block : block + 1], (128, 128)) * place
        gain_rows = jnp.broadcast_to(columns[:, block + 4 : block + 5], (128, 128))
        up = jnp.exp(power)
        down = jnp.exp(-power)
        powers[rows, 0:128] = down
        powers[rows, 128:256] = up
        gains[rows, 0:128] = gain_rows * up
        gains[rows, 128:256] = gain_rows * down
    log_block = log_root * 128.0
    group_decay = jnp.exp(log_block * float(XG))
    image_sum = 1.0 - jnp.exp(log_block * float(nlon))

    for row in range(8, 536, RH):
        delta[0, pl.ds(row, RH)] = jnp.zeros((RH, 128), F32)
        delta[1, pl.ds(row, RH)] = jnp.zeros((RH, 128), F32)

    first_half = lax.rem(lane8, 16) < 8
    def set_west(rows, outer):
        inner = main[WEST, rows]
        first = iota(inner.shape, 1) == 0
        main[WEST, rows] = jnp.where(first, outer, inner)
        halo[WEST, rows] = jnp.where(first, inner, outer)

    for block in range(4):
        own = pl.ds(128 * block + PAD, 128)
        to_west[block].wait_recv()
        to_east[block].wait_recv()
        edges = strip_in[block].reshape(128, 128).T
        for field in range(FIELDS):
            halo[field, own] = roll(edges, -16 * (field + 1), 1)
        set_west(own, roll(edges, 1 - 16 * 3, 1))

    @pl.when(jnp.logical_not(low))
    def _():
        to_north.wait_recv()
        to_nw.wait_recv()
        to_ne.wait_recv()

    south_corner = jnp.where(first_half, corner[1], corner[0])
    for field in range(FIELDS):
        halo[field, pl.ds(8, 8)] = roll(south_corner, -16 * (field + 1), 1)
    to_south.wait_recv()
    to_sw.wait_recv()
    to_se.wait_recv()

    @pl.when(top)
    def _():
        over_fold.wait_send()

    @pl.when(jnp.logical_not(top))
    def _():
        to_north.wait_send()

    @pl.when(jnp.logical_not(low))
    def _():
        to_south.wait_send()

    @pl.when(jnp.logical_not(top))
    def _():
        north_corner = jnp.where(first_half, corner[3], corner[2])
        for field in range(FIELDS):
            halo[field, pl.ds(PAD + 512, 8)] = roll(north_corner, -16 * (field + 1), 1)

    @pl.when(top)
    def _():
        mixed = jnp.where(first_half, corner[2], corner[3])
        tiles = [main[field, pl.ds(PAD + 512, 8)] for field in range(FIELDS)] + [mixed, zero8]
        stack = jnp.concatenate(tiles, axis=0)
        flip = (iota((128, 128), 0) + iota((128, 128), 1) == 127).astype(F32)
        row_to = iota((64, 64), 0)
        row_from = iota((64, 64), 1)
        swap = (row_to // 8 == row_from // 8) & (row_to % 8 + row_from % 8 == 7)
        turned = jnp.dot(stack, flip, precision=HIGH, preferred_element_type=F32)
        turned = jnp.dot(swap.astype(F32), turned, precision=HIGH, preferred_element_type=F32)
        ghost = pl.ds(PAD + 512, 8)
        for field in range(FIELDS):
            inner = turned[8 * field : 8 * field + 8]
            outer = roll(turned[48:56], 16 * (field + 1), 1)
            if field == 2:
                inner, outer = roll(inner, -1, 1), roll(outer, -1, 1)
                inner, outer = (
                    jnp.where(lane8 == 127, outer, inner),
                    jnp.where(lane8 == 127, inner, outer),
                )
            if field == 3:
                last = pl.ds(PAD + 504, 8)
                main[3, last] = jnp.where(sub8 == 7, main[3, last] * inner[0:1], main[3, last])
                halo[3, last] = jnp.where(sub8 == 7, halo[3, last] * outer[0:1], halo[3, last])
                inner, outer = roll(inner, -1, 0), roll(outer, -1, 0)
            main[field, ghost] = inner
            halo[field, ghost] = outer

    for edge in (8, PAD + 512):
        rows = pl.ds(edge, 8)
        main[WEST, rows] = roll(main[2, rows], 1, 1)
        set_west(rows, roll(halo[2, rows], 1, 1))

    last_lane = iota((RH, 128), 1) == 127
    zero_lane = iota((RH, 128), 1) == 0

    def substep(src, dst):
        for row in range(8, 536, RH):
            here, up, down = pl.ds(row, RH), pl.ds(row + 1, RH), pl.ds(row - 1, RH)
            states = [src[side][here] for side in range(2)]
            east = [roll(state, -1, 1) for state in states]
            west = [roll(state, 1, 1) for state in states]
            for side, field in enumerate((main, halo)):
                state = states[side]
                to_east = jnp.where(last_lane, east[1 - side], east[side]) - state
                to_west = jnp.where(zero_lane, west[1 - side], west[side]) - state
                spread = field[2, here] * to_east + field[WEST, here] * to_west
                spread = spread + field[3, here] * (src[side][up] - state)
                spread = spread + field[3, down] * (src[side][down] - state)
                change = delta[side, here] + field[1, here] * spread
                delta[side, here] = change
                dst[side][here] = state + change

    side_a = (main.at[0], halo.at[0])
    side_b = (work.at[0], work.at[1])

    def forward_pair(step, carry):
        substep(side_a, side_b)
        substep(side_b, side_a)
        return carry

    lax.fori_loop(0, SUBSTEPS // 2, forward_pair, 0)

    for row in range(8, 536, RH):
        here = pl.ds(row, RH)
        for side, field in enumerate((main, halo)):
            start = field[1, here] * field[4, here] * (field[0, here] - field[5, here])
            work[side, here] = start
            delta[side, here] = start
    eta_ref[...] = main[0, pl.ds(PAD, 512)]

    def adjoint_pair(step, carry):
        substep(side_b, side_a)
        substep(side_a, side_b)
        return carry

    lax.fori_loop(0, SUBSTEPS // 2, adjoint_pair, 0)

    ends = jnp.zeros((8, 128), F32)
    pick_row = iota((8, 256), 0)
    pick_half = 4 * (iota((8, 256), 1) // 128)
    for block in range(4):
        rows = pl.ds(block * 128, 128)
        gradient = delta[0, pl.ds(PAD + block * 128, 128)] / raw_f[0, rows]
        both_ways = jnp.concatenate(
            [gradient * powers[rows, 0:128], gradient * powers[rows, 128:256]], axis=1
        )
        pick = (pick_row == pick_half + block).astype(BF16)
        for index, part in enumerate(split3(both_ways)):
            parts[index, rows] = part
            ends = ends + lax.dot_general(
                pick, part, (((1,), (1,)), ((), ())), preferred_element_type=F32
            )

    forward_half = sub8 < 4
    to_end, reach = [], []
    for step in range(XG):
        source = lax.rem(x_pos + XG - step, XG)
        blocks = jnp.where(forward_half, XG - 1 - source, source).astype(F32)
        to_end.append(jnp.exp(log_block * blocks))
        ahead = jnp.where(forward_half, x_pos - source, source - x_pos)
        near = jnp.exp(log_block * jnp.maximum(ahead, 1).astype(F32))
        reach.append(jnp.where(ahead > 0, near, 0.0))
    steps_in = jnp.where(forward_half, x_pos, XG - 1 - x_pos).astype(F32)
    group_weight = jnp.exp(log_block * (steps_in + 1.0)) / image_sum
    for step in range(1, nz + 1):
        z_weight[step - 1] = group_weight
        group_weight = group_weight * group_decay
    xbuf[0] = ends
    x_copies = [
        remote(xbuf.at[0], xbuf.at[step], xs.at[step - 1], xr.at[step - 1], x_peer(step), lat)
        for step in (2, 1, 3)
    ]
    for copy in x_copies:
        copy.start()

    for copy in x_copies:
        copy.wait_recv()
    tiles = [xbuf[step] for step in range(XG)]
    group = sum(to_end[step] * tiles[step] for step in range(XG))
    zbuf[0] = group
    z_copies = [
        remote(zbuf.at[0], zbuf.at[step], zs.at[step - 1], zr.at[step - 1], z_peer(step), lat)
        for step in far_first
    ]
    for copy in z_copies:
        copy.start()

    col = iota((256, 256), 1)
    row = iota((256, 256), 0)
    ahead = ((row < 128) & (col < 128) & (row <= col)) | ((row >= 128) & (col >= 128) & (row > col))
    ahead = ahead.astype(F32).astype(BF16)
    for block in range(4):
        rows = pl.ds(block * 128, 128)
        total = jnp.dot(parts[0, rows], ahead, preferred_element_type=F32)
        total = total + jnp.dot(parts[1, rows], ahead, preferred_element_type=F32)
        sums[rows] = total + jnp.dot(parts[2, rows], ahead, preferred_element_type=F32)

    inside = sum(reach[step] * tiles[step] for step in range(XG))
    for block in range(4):
        rows = pl.ds(block * 128, 128)
        both_gains = gains[rows]
        both_sums = both_gains * sums[rows]
        grad_ref[rows] = both_sums[:, 0:128] + both_sums[:, 128:256]

    for copy in z_copies:
        copy.wait_recv()
    terms = [inside]
    for step in range(1, nz + 1):
        tile = jnp.where(forward_half, zbuf[step % nz], zbuf[(nz - step) % nz])
        terms.append(z_weight[step - 1] * tile)
    while len(terms) > 1:
        terms = [a + b for a, b in zip(terms[::2], terms[1::2])] + terms[len(terms) // 2 * 2 :]
    inflow = terms[0]
    inflow_cols = jnp.concatenate([inflow] * 16, axis=0).T
    for block in range(4):
        rows = pl.ds(block * 128, 128)
        east_in = jnp.broadcast_to(inflow_cols[:, block : block + 1], (128, 128))
        west_in = jnp.broadcast_to(inflow_cols[:, block + 4 : block + 5], (128, 128))
        inner = gains[rows, 0:128] * east_in + gains[rows, 128:256] * west_in
        grad_ref[rows] = grad_ref[rows] + inner

    for copy in to_west + to_east:
        copy.wait_send()

    @pl.when(top)
    def _():
        @pl.when(jnp.logical_not(nw_self))
        def _():
            fold_to_nw.wait_send()

        @pl.when(jnp.logical_not(ne_self))
        def _():
            fold_to_ne.wait_send()

    @pl.when(jnp.logical_not(top))
    def _():
        to_nw.wait_send()
        to_ne.wait_send()

    @pl.when(jnp.logical_not(low))
    def _():
        to_sw.wait_send()
        to_se.wait_send()

    for copy in x_copies:
        copy.wait_send()
    for copy in z_copies:
        copy.wait_send()


def write_out(eta_ref, grad_ref, eta_hbm, grad_hbm, sem):
    copies = []
    for index, (src, dst) in enumerate(((eta_ref, eta_hbm), (grad_ref, grad_hbm))):
        for part in range(4):
            rows = pl.ds(part * 128, 128)
            copies.append(pltpu.make_async_copy(src.at[rows], dst.at[rows], sem.at[index, part]))
    for copy in copies:
        copy.start()
    for copy in copies:
        copy.wait()


def local(
    wet_mask, east_level, north_level, courant, increment, innovation, obs_weight, smooth_scale
):
    nlon = lax.axis_size("lon")
    nlat = lax.axis_size("lat")
    nz = nlon // XG
    hbm = pl.BlockSpec(memory_space=pltpu.MemorySpace.HBM)
    vmem = pl.BlockSpec(memory_space=pltpu.VMEM)
    dma = pltpu.SemaphoreType.DMA
    block = jax.ShapeDtypeStruct((512, 128), F32)
    eta, gradient = pl.pallas_call(
        functools.partial(kernel, nlon, nlat),
        out_shape=(block, block),
        in_specs=[hbm] * 8,
        out_specs=(vmem, vmem),
        scratch_shapes=[
            pltpu.VMEM((3, 512, 128), jnp.int32),
            pltpu.VMEM((2, 512, 128), F32),
            pltpu.VMEM((FIELDS + 1, 544, 128), F32),
            pltpu.VMEM((FIELDS + 1, 544, 128), F32),
            pltpu.VMEM((2, 544, 128), F32),
            pltpu.VMEM((2, 544, 128), F32),
            pltpu.VMEM((512, 128), F32),
            pltpu.VMEM((4, 8, 2, 8, 128), F32),
            pltpu.VMEM((4, 8, 2, 8, 128), F32),
            pltpu.VMEM((4, 8, 128), F32),
            pltpu.VMEM((4, 128), F32),
            pltpu.VMEM((512, 256), F32),
            pltpu.VMEM((512, 256), F32),
            pltpu.VMEM((3, 512, 256), BF16),
            pltpu.VMEM((512, 256), F32),
            pltpu.VMEM((XG, 8, 128), F32),
            pltpu.VMEM((nz, 8, 128), F32),
            pltpu.VMEM((nz, 8, 128), F32),
            dma((8,)),
            dma((16,)),
            dma((16,)),
            dma((XG - 1,)),
            dma((XG - 1,)),
            dma((nz - 1,)),
            dma((nz - 1,)),
        ],
        compiler_params=pltpu.CompilerParams(
            collective_id=0, has_side_effects=True, vmem_limit_bytes=54656 * 1024
        ),
    )(
        wet_mask,
        east_level,
        north_level,
        courant,
        increment,
        innovation,
        obs_weight,
        smooth_scale.reshape(4, 128),
    )
    return pl.pallas_call(
        write_out,
        out_shape=(block, block),
        in_specs=[vmem] * 2,
        out_specs=(hbm, hbm),
        scratch_shapes=[dma((2, 4))],
        compiler_params=pltpu.CompilerParams(vmem_limit_bytes=1024 * 1024),
    )(eta, gradient)


def solution(mesh):
    return jax.shard_map(
        local,
        mesh=mesh,
        in_specs=(P("lat", "lon"),) * 7 + (P("lat"),),
        out_specs=(P("lat", "lon"), P("lat", "lon")),
        check_vma=False,
    )
```

```python
import functools
import jax
import jax.numpy as jnp
from jax import lax
from jax.experimental import pallas as pl
from jax.experimental.pallas import tpu as pltpu
from jax.sharding import PartitionSpec as P

SUBSTEPS = 4
WLEV = 8
F32 = jnp.float32
BF16 = jnp.bfloat16
XG = 4
FIELDS = 6
WEST = 6
PAD = 16
RH = 24
HIGH = lax.Precision.HIGHEST


def roll(value, shift, axis):
    return pltpu.roll(value, shift % value.shape[axis], axis)


def iota(shape, dim):
    return lax.broadcasted_iota(jnp.int32, shape, dim)


def split3(value):
    high = value.astype(BF16)
    rest = value - high.astype(F32)
    mid = rest.astype(BF16)
    low = (rest - mid.astype(F32)).astype(BF16)
    return high, mid, low


def remote(src, dst, send_sem, recv_sem, lon, lat):
    return pltpu.make_async_remote_copy(
        src_ref=src,
        dst_ref=dst,
        send_sem=send_sem,
        recv_sem=recv_sem,
        device_id={"lon": lon, "lat": lat},
        device_id_type=pl.DeviceIdType.MESH,
    )


def kernel(
    nlon,
    nlat,
    wet_hbm,
    east_hbm,
    north_hbm,
    cour_hbm,
    incr_hbm,
    innov_hbm,
    ow_hbm,
    scale_hbm,
    eta_ref,
    grad_ref,
    raw_i,
    raw_f,
    main,
    halo,
    work,
    delta,
    packed,
    strip_out,
    strip_in,
    corner,
    scale_buf,
    powers,
    gains,
    parts,
    sums,
    xbuf,
    zbuf,
    z_weight,
    known,
    in_sem,
    hs,
    hr,
    xs,
    xr,
    zs,
    zr,
):
    lon = lax.axis_index("lon")
    lat = lax.axis_index("lat")
    nz = nlon // XG
    x_pos = lax.rem(lon, XG)
    z_pos = lon // XG
    top = lat == nlat - 1
    low = lat == 0
    east_lon = lax.rem(lon + 1, nlon)
    west_lon = lax.rem(lon + nlon - 1, nlon)
    fold_lon = nlon - 1 - lon
    fold_ne = lax.rem(2 * nlon - 2 - lon, nlon)
    fold_nw = lax.rem(nlon - lon, nlon)
    ne_self = fold_ne == lon
    nw_self = fold_nw == lon

    loads = [
        pltpu.make_async_copy(scale_hbm, scale_buf, in_sem.at[7]),
        pltpu.make_async_copy(wet_hbm, raw_i.at[0], in_sem.at[0]),
        pltpu.make_async_copy(cour_hbm, raw_f.at[0], in_sem.at[1]),
        pltpu.make_async_copy(incr_hbm, raw_f.at[1], in_sem.at[2]),
        pltpu.make_async_copy(east_hbm, raw_i.at[1], in_sem.at[3]),
        pltpu.make_async_copy(north_hbm, raw_i.at[2], in_sem.at[4]),
        pltpu.make_async_copy(ow_hbm, main.at[4, pl.ds(PAD, 512)], in_sem.at[5]),
        pltpu.make_async_copy(innov_hbm, main.at[5, pl.ds(PAD, 512)], in_sem.at[6]),
    ]
    barrier = pltpu.get_barrier_semaphore()

    def greet(to_lon, to_lat):
        pl.semaphore_signal(
            barrier,
            inc=1,
            device_id={"lon": to_lon, "lat": to_lat},
            device_id_type=pl.DeviceIdType.MESH,
        )

    def x_peer(step):
        return z_pos * XG + lax.rem(x_pos + step, XG)

    def z_peer(step):
        return lax.rem(z_pos + step, nz) * XG + x_pos

    greet(east_lon, lat)
    greet(west_lon, lat)

    @pl.when(jnp.logical_not(low))
    def _():
        greet(lon, lat - 1)
        greet(east_lon, lat - 1)
        greet(west_lon, lat - 1)

    @pl.when(jnp.logical_not(top))
    def _():
        greet(lon, lat + 1)
        greet(east_lon, lat + 1)
        greet(west_lon, lat + 1)

    @pl.when(top)
    def _():
        greet(fold_lon, lat)

        @pl.when(jnp.logical_not(ne_self))
        def _():
            greet(fold_ne, lat)

        @pl.when(jnp.logical_not(nw_self))
        def _():
            greet(fold_nw, lat)

    for load in loads:
        load.start()
    far_first = sorted(range(1, nz), key=lambda step: -min(step, nz - step))
    for step in (1, nz - 1):
        greet(z_peer(step), lat)
    for step in range(1, XG):
        greet(x_peer(step), lat)

    lane8 = iota((8, 128), 1)
    sub8 = iota((8, 128), 0)

    zero8 = jnp.zeros((8, 128), F32)
    for block in range(4):
        for slot, side in ((0, 0), (6, 1), (7, 0), (7, 1)):
            strip_in[block, slot, side] = zero8
    for edge in (0, 536):
        for field in (0, 3):
            main[field, pl.ds(edge, 8)] = zero8
            halo[field, pl.ds(edge, 8)] = zero8
        work[0, pl.ds(edge, 8)] = zero8
        work[1, pl.ds(edge, 8)] = zero8

    @pl.when(low)
    def _():
        for field in range(FIELDS):
            main[field, pl.ds(8, 8)] = zero8
        corner[0] = zero8
        corner[1] = zero8

    for load in loads:
        load.wait()
    slot = (iota((32, 128), 1) + 8) // 16
    for block in range(4):
        for row in range(128 * block, 128 * block + 128, 32):
            rows, own = pl.ds(row, 32), pl.ds(row + PAD, 32)
            wet = raw_i[0, rows].astype(F32)
            fields = [
                wet * raw_f[1, rows],
                wet * raw_f[0, rows],
                raw_i[1, rows].astype(F32) * (1.0 / WLEV),
                raw_i[2, rows].astype(F32) * (1.0 / WLEV),
            ]
            for index, value in enumerate(fields):
                main[index, own] = value
            main[WEST, own] = roll(fields[2], 1, 1)
            fields.append(main[4, own])
            fields.append(main[5, own])
            joined = roll(fields[0], 16, 1)
            for index in range(1, FIELDS):
                moved = roll(fields[index], 16 * (index + 1), 1)
                joined = jnp.where(slot == index + 1, moved, joined)
            packed[rows] = joined

    links = 2 + (XG - 1) + 2
    north_links = jnp.where(
        top, 3 - ne_self.astype(jnp.int32) - nw_self.astype(jnp.int32), 3
    )
    south_links = jnp.where(low, 0, 3)
    pl.semaphore_wait(barrier, links + north_links + south_links)

    rounds = nz.bit_length() - 2

    def pass_on(index):
        for step in (2**index, nz - 2**index):
            pl.semaphore_signal(
                known.at[index],
                inc=1,
                device_id={"lon": z_peer(step), "lat": lat},
                device_id_type=pl.DeviceIdType.MESH,
            )

    def hear(index):
        pl.semaphore_wait(known.at[index], 2)
        if index + 1 < rounds:
            pass_on(index + 1)

    pass_on(0)

    top_rows = main.at[pl.ds(0, FIELDS), pl.ds(PAD + 504, 8)]
    low_rows = main.at[pl.ds(0, FIELDS), pl.ds(PAD, 8)]
    south_halo = main.at[pl.ds(0, FIELDS), pl.ds(8, 8)]
    north_halo = main.at[pl.ds(0, FIELDS), pl.ds(PAD + 512, 8)]
    top_tile = packed.at[pl.ds(504, 8)]
    low_tile = packed.at[pl.ds(0, 8)]
    to_west, to_east = [], []
    for block in range(4):
        first = strip_out.at[block, pl.ds(1, 6), 0], strip_in.at[block, pl.ds(1, 6), 0]
        last = strip_out.at[block, pl.ds(0, 6), 1], strip_in.at[block, pl.ds(0, 6), 1]
        to_west.append(remote(*first, hs.at[8 + block], hr.at[8 + block], west_lon, lat))
        to_east.append(remote(*last, hs.at[12 + block], hr.at[12 + block], east_lon, lat))
    to_south = remote(low_rows, north_halo, hs.at[0], hr.at[1], lon, lat - 1)
    to_sw = remote(low_tile, corner.at[3], hs.at[4], hr.at[7], west_lon, lat - 1)
    to_se = remote(low_tile, corner.at[2], hs.at[5], hr.at[6], east_lon, lat - 1)
    to_north = remote(top_rows, south_halo, hs.at[1], hr.at[0], lon, lat + 1)
    to_nw = remote(top_tile, corner.at[1], hs.at[6], hr.at[5], west_lon, lat + 1)
    to_ne = remote(top_tile, corner.at[0], hs.at[7], hr.at[4], east_lon, lat + 1)
    over_fold = remote(top_rows, north_halo, hs.at[1], hr.at[1], fold_lon, lat)
    fold_to_nw = remote(top_tile, corner.at[2], hs.at[6], hr.at[6], fold_nw, lat)
    fold_to_ne = remote(top_tile, corner.at[3], hs.at[7], hr.at[7], fold_ne, lat)
    own_nw = pltpu.make_async_copy(top_tile, corner.at[2], hr.at[6])
    own_ne = pltpu.make_async_copy(top_tile, corner.at[3], hr.at[7])

    @pl.when(top)
    def _():
        over_fold.start()

        @pl.when(jnp.logical_not(nw_self))
        def _():
            fold_to_nw.start()

        @pl.when(nw_self)
        def _():
            own_nw.start()

        @pl.when(jnp.logical_not(ne_self))
        def _():
            fold_to_ne.start()

        @pl.when(ne_self)
        def _():
            own_ne.start()

    @pl.when(jnp.logical_not(top))
    def _():
        to_north.start()
        to_nw.start()
        to_ne.start()

    @pl.when(jnp.logical_not(low))
    def _():
        to_south.start()
        to_sw.start()
        to_se.start()

    for block in range(4):
        turned = packed[pl.ds(128 * block, 128)].T
        strip_out[block] = turned.reshape(8, 2, 8, 128)
        to_west[block].start()
        to_east[block].start()

    scale = scale_buf[...]
    scale = jnp.concatenate([scale, scale], axis=0)
    stiff = scale * float(128 * 128)
    root_term = jnp.sqrt(1.0 + 4.0 * stiff)
    log_root = jnp.log1p(-(root_term - 1.0) / (2.0 * stiff))
    gain = (1.0 / root_term) * (2.0 * jnp.sqrt(jnp.sqrt(stiff)))
    both = jnp.where(sub8 < 4, log_root, gain)
    columns = jnp.concatenate([both] * 16, axis=0).T
    place = iota((128, 128), 1).astype(F32) - 63.5
    for block in range(4):
        rows = pl.ds(block * 128, 128)
        power = jnp.broadcast_to(columns[:, block : block + 1], (128, 128)) * place
        gain_rows = jnp.broadcast_to(columns[:, block + 4 : block + 5], (128, 128))
        up = jnp.exp(power)
        down = jnp.exp(-power)
        powers[rows, 0:128] = down
        powers[rows, 128:256] = up
        gains[rows, 0:128] = gain_rows * up
        gains[rows, 128:256] = gain_rows * down
    log_block = log_root * 128.0
    group_decay = jnp.exp(log_block * float(XG))
    image_sum = 1.0 - jnp.exp(log_block * float(nlon))

    for row in range(8, 536, RH):
        delta[0, pl.ds(row, RH)] = jnp.zeros((RH, 128), F32)
        delta[1, pl.ds(row, RH)] = jnp.zeros((RH, 128), F32)

    hear(0)

    first_half = lax.rem(lane8, 16) < 8
    def set_west(rows, outer):
        inner = main[WEST, rows]
        first = iota(inner.shape, 1) == 0
        main[WEST, rows] = jnp.where(first, outer, inner)
        halo[WEST, rows] = jnp.where(first, inner, outer)

    for block in range(4):
        own = pl.ds(128 * block + PAD, 128)
        to_west[block].wait_recv()
        to_east[block].wait_recv()
        edges = strip_in[block].reshape(128, 128).T
        for field in range(FIELDS):
            halo[field, own] = roll(edges, -16 * (field + 1), 1)
        set_west(own, roll(edges, 1 - 16 * 3, 1))

    @pl.when(jnp.logical_not(low))
    def _():
        to_north.wait_recv()
        to_nw.wait_recv()
        to_ne.wait_recv()

    south_corner = jnp.where(first_half, corner[1], corner[0])
    for field in range(FIELDS):
        halo[field, pl.ds(8, 8)] = roll(south_corner, -16 * (field + 1), 1)
    to_south.wait_recv()
    to_sw.wait_recv()
    to_se.wait_recv()

    @pl.when(top)
    def _():
        over_fold.wait_send()

    @pl.when(jnp.logical_not(top))
    def _():
        to_north.wait_send()

    @pl.when(jnp.logical_not(low))
    def _():
        to_south.wait_send()

    @pl.when(jnp.logical_not(top))
    def _():
        north_corner = jnp.where(first_half, corner[3], corner[2])
        for field in range(FIELDS):
            halo[field, pl.ds(PAD + 512, 8)] = roll(north_corner, -16 * (field + 1), 1)

    @pl.when(top)
    def _():
        mixed = jnp.where(first_half, corner[2], corner[3])
        tiles = [main[field, pl.ds(PAD + 512, 8)] for field in range(FIELDS)] + [mixed, zero8]
        stack = jnp.concatenate(tiles, axis=0)
        flip = (iota((128, 128), 0) + iota((128, 128), 1) == 127).astype(F32)
        row_to = iota((64, 64), 0)
        row_from = iota((64, 64), 1)
        swap = (row_to // 8 == row_from // 8) & (row_to % 8 + row_from % 8 == 7)
        turned = jnp.dot(stack, flip, precision=HIGH, preferred_element_type=F32)
        turned = jnp.dot(swap.astype(F32), turned, precision=HIGH, preferred_element_type=F32)
        ghost = pl.ds(PAD + 512, 8)
        for field in range(FIELDS):
            inner = turned[8 * field : 8 * field + 8]
            outer = roll(turned[48:56], 16 * (field + 1), 1)
            if field == 2:
                inner, outer = roll(inner, -1, 1), roll(outer, -1, 1)
                inner, outer = (
                    jnp.where(lane8 == 127, outer, inner),
                    jnp.where(lane8 == 127, inner, outer),
                )
            if field == 3:
                last = pl.ds(PAD + 504, 8)
                main[3, last] = jnp.where(sub8 == 7, main[3, last] * inner[0:1], main[3, last])
                halo[3, last] = jnp.where(sub8 == 7, halo[3, last] * outer[0:1], halo[3, last])
                inner, outer = roll(inner, -1, 0), roll(outer, -1, 0)
            main[field, ghost] = inner
            halo[field, ghost] = outer

    for edge in (8, PAD + 512):
        rows = pl.ds(edge, 8)
        main[WEST, rows] = roll(main[2, rows], 1, 1)
        set_west(rows, roll(halo[2, rows], 1, 1))

    last_lane = iota((RH, 128), 1) == 127
    zero_lane = iota((RH, 128), 1) == 0

    def substep(src, dst):
        for row in range(8, 536, RH):
            here, up, down = pl.ds(row, RH), pl.ds(row + 1, RH), pl.ds(row - 1, RH)
            states = [src[side][here] for side in range(2)]
            east = [roll(state, -1, 1) for state in states]
            west = [roll(state, 1, 1) for state in states]
            for side, field in enumerate((main, halo)):
                state = states[side]
                to_east = jnp.where(last_lane, east[1 - side], east[side]) - state
                to_west = jnp.where(zero_lane, west[1 - side], west[side]) - state
                spread = field[2, here] * to_east + field[WEST, here] * to_west
                spread = spread + field[3, here] * (src[side][up] - state)
                spread = spread + field[3, down] * (src[side][down] - state)
                change = delta[side, here] + field[1, here] * spread
                delta[side, here] = change
                dst[side][here] = state + change

    side_a = (main.at[0], halo.at[0])
    side_b = (work.at[0], work.at[1])

    def forward_pair(step, carry):
        substep(side_a, side_b)
        substep(side_b, side_a)
        return carry

    lax.fori_loop(0, SUBSTEPS // 2, forward_pair, 0)

    for row in range(8, 536, RH):
        here = pl.ds(row, RH)
        for side, field in enumerate((main, halo)):
            start = field[1, here] * field[4, here] * (field[0, here] - field[5, here])
            work[side, here] = start
            delta[side, here] = start
    eta_ref[...] = main[0, pl.ds(PAD, 512)]

    if rounds > 1:
        hear(1)

    def adjoint_pair(step, carry):
        substep(side_b, side_a)
        substep(side_a, side_b)
        return carry

    lax.fori_loop(0, SUBSTEPS // 2, adjoint_pair, 0)

    ends = jnp.zeros((8, 128), F32)
    pick_row = iota((8, 256), 0)
    pick_half = 4 * (iota((8, 256), 1) // 128)
    for block in range(4):
        rows = pl.ds(block * 128, 128)
        gradient = delta[0, pl.ds(PAD + block * 128, 128)] / raw_f[0, rows]
        both_ways = jnp.concatenate(
            [gradient * powers[rows, 0:128], gradient * powers[rows, 128:256]], axis=1
        )
        pick = (pick_row == pick_half + block).astype(BF16)
        for index, part in enumerate(split3(both_ways)):
            parts[index, rows] = part
            ends = ends + lax.dot_general(
                pick, part, (((1,), (1,)), ((), ())), preferred_element_type=F32
            )

    forward_half = sub8 < 4
    to_end, reach = [], []
    for step in range(XG):
        source = lax.rem(x_pos + XG - step, XG)
        blocks = jnp.where(forward_half, XG - 1 - source, source).astype(F32)
        to_end.append(jnp.exp(log_block * blocks))
        ahead = jnp.where(forward_half, x_pos - source, source - x_pos)
        near = jnp.exp(log_block * jnp.maximum(ahead, 1).astype(F32))
        reach.append(jnp.where(ahead > 0, near, 0.0))
    steps_in = jnp.where(forward_half, x_pos, XG - 1 - x_pos).astype(F32)
    group_weight = jnp.exp(log_block * (steps_in + 1.0)) / image_sum
    for step in range(1, nz + 1):
        z_weight[step - 1] = group_weight
        group_weight = group_weight * group_decay
    xbuf[0] = ends
    x_copies = [
        remote(xbuf.at[0], xbuf.at[step], xs.at[step - 1], xr.at[step - 1], x_peer(step), lat)
        for step in (2, 1, 3)
    ]
    for copy in x_copies:
        copy.start()

    for copy in x_copies:
        copy.wait_recv()
    tiles = [xbuf[step] for step in range(XG)]
    group = sum(to_end[step] * tiles[step] for step in range(XG))
    zbuf[0] = group
    z_copies = [
        remote(zbuf.at[0], zbuf.at[step], zs.at[step - 1], zr.at[step - 1], z_peer(step), lat)
        for step in far_first
    ]
    for index in range(2, rounds):
        hear(index)
    for copy in z_copies:
        copy.start()

    col = iota((256, 256), 1)
    row = iota((256, 256), 0)
    ahead = ((row < 128) & (col < 128) & (row <= col)) | ((row >= 128) & (col >= 128) & (row > col))
    ahead = ahead.astype(F32).astype(BF16)
    for block in range(4):
        rows = pl.ds(block * 128, 128)
        total = jnp.dot(parts[0, rows], ahead, preferred_element_type=F32)
        total = total + jnp.dot(parts[1, rows], ahead, preferred_element_type=F32)
        sums[rows] = total + jnp.dot(parts[2, rows], ahead, preferred_element_type=F32)

    inside = sum(reach[step] * tiles[step] for step in range(XG))
    for block in range(4):
        rows = pl.ds(block * 128, 128)
        both_gains = gains[rows]
        both_sums = both_gains * sums[rows]
        grad_ref[rows] = both_sums[:, 0:128] + both_sums[:, 128:256]

    for copy in z_copies:
        copy.wait_recv()
    terms = [inside]
    for step in range(1, nz + 1):
        tile = jnp.where(forward_half, zbuf[step % nz], zbuf[(nz - step) % nz])
        terms.append(z_weight[step - 1] * tile)
    while len(terms) > 1:
        terms = [a + b for a, b in zip(terms[::2], terms[1::2])] + terms[len(terms) // 2 * 2 :]
    inflow = terms[0]
    inflow_cols = jnp.concatenate([inflow] * 16, axis=0).T
    for block in range(4):
        rows = pl.ds(block * 128, 128)
        east_in = jnp.broadcast_to(inflow_cols[:, block : block + 1], (128, 128))
        west_in = jnp.broadcast_to(inflow_cols[:, block + 4 : block + 5], (128, 128))
        inner = gains[rows, 0:128] * east_in + gains[rows, 128:256] * west_in
        grad_ref[rows] = grad_ref[rows] + inner

    for copy in to_west + to_east:
        copy.wait_send()

    @pl.when(top)
    def _():
        @pl.when(jnp.logical_not(nw_self))
        def _():
            fold_to_nw.wait_send()

        @pl.when(jnp.logical_not(ne_self))
        def _():
            fold_to_ne.wait_send()

    @pl.when(jnp.logical_not(top))
    def _():
        to_nw.wait_send()
        to_ne.wait_send()

    @pl.when(jnp.logical_not(low))
    def _():
        to_sw.wait_send()
        to_se.wait_send()

    for copy in x_copies:
        copy.wait_send()
    for copy in z_copies:
        copy.wait_send()


def write_out(eta_ref, grad_ref, eta_hbm, grad_hbm, sem):
    copies = []
    for index, (src, dst) in enumerate(((eta_ref, eta_hbm), (grad_ref, grad_hbm))):
        for part in range(4):
            rows = pl.ds(part * 128, 128)
            copies.append(pltpu.make_async_copy(src.at[rows], dst.at[rows], sem.at[index, part]))
    for copy in copies:
        copy.start()
    for copy in copies:
        copy.wait()


def local(
    wet_mask, east_level, north_level, courant, increment, innovation, obs_weight, smooth_scale
):
    nlon = lax.axis_size("lon")
    nlat = lax.axis_size("lat")
    nz = nlon // XG
    inputs = (
        wet_mask,
        east_level,
        north_level,
        courant,
        increment,
        innovation,
        obs_weight,
        smooth_scale.reshape(4, 128),
    )
    hbm = pl.BlockSpec(memory_space=pltpu.MemorySpace.HBM)
    vmem = pl.BlockSpec(memory_space=pltpu.VMEM)
    dma = pltpu.SemaphoreType.DMA
    block = jax.ShapeDtypeStruct((512, 128), F32)
    eta, gradient = pl.pallas_call(
        functools.partial(kernel, nlon, nlat),
        out_shape=(block, block),
        in_specs=[hbm] * 8,
        out_specs=(vmem, vmem),
        scratch_shapes=[
            pltpu.VMEM((3, 512, 128), jnp.int32),
            pltpu.VMEM((2, 512, 128), F32),
            pltpu.VMEM((FIELDS + 1, 544, 128), F32),
            pltpu.VMEM((FIELDS + 1, 544, 128), F32),
            pltpu.VMEM((2, 544, 128), F32),
            pltpu.VMEM((2, 544, 128), F32),
            pltpu.VMEM((512, 128), F32),
            pltpu.VMEM((4, 8, 2, 8, 128), F32),
            pltpu.VMEM((4, 8, 2, 8, 128), F32),
            pltpu.VMEM((4, 8, 128), F32),
            pltpu.VMEM((4, 128), F32),
            pltpu.VMEM((512, 256), F32),
            pltpu.VMEM((512, 256), F32),
            pltpu.VMEM((3, 512, 256), BF16),
            pltpu.VMEM((512, 256), F32),
            pltpu.VMEM((XG, 8, 128), F32),
            pltpu.VMEM((nz, 8, 128), F32),
            pltpu.VMEM((nz, 8, 128), F32),
            pltpu.SemaphoreType.REGULAR((nz.bit_length() - 2,)),
            dma((8,)),
            dma((16,)),
            dma((16,)),
            dma((XG - 1,)),
            dma((XG - 1,)),
            dma((nz - 1,)),
            dma((nz - 1,)),
        ],
        compiler_params=pltpu.CompilerParams(
            collective_id=0, has_side_effects=True, vmem_limit_bytes=32 * 1024 * 1024
        ),
    )(*[pltpu.with_memory_space_constraint(value, pltpu.MemorySpace.HBM) for value in inputs])
    return pl.pallas_call(
        write_out,
        out_shape=(block, block),
        in_specs=[vmem] * 2,
        out_specs=(hbm, hbm),
        scratch_shapes=[dma((2, 4))],
        compiler_params=pltpu.CompilerParams(vmem_limit_bytes=1024 * 1024),
    )(eta, gradient)


def solution(mesh):
    return jax.shard_map(
        local,
        mesh=mesh,
        in_specs=(P("lat", "lon"),) * 7 + (P("lat"),),
        out_specs=(P("lat", "lon"), P("lat", "lon")),
        check_vma=False,
    )
```

```python
import functools
import jax
import jax.numpy as jnp
from jax import lax
from jax.experimental import pallas as pl
from jax.experimental.pallas import tpu as pltpu
from jax.sharding import PartitionSpec as P

SUBSTEPS = 4
WLEV = 8
F32 = jnp.float32
BF16 = jnp.bfloat16
XG = 4
FIELDS = 6
WEST = 6
PAD = 16
RH = 24
HIGH = lax.Precision.HIGHEST


def roll(value, shift, axis):
    return pltpu.roll(value, shift % value.shape[axis], axis)


def iota(shape, dim):
    return lax.broadcasted_iota(jnp.int32, shape, dim)


def split3(value):
    high = value.astype(BF16)
    rest = value - high.astype(F32)
    mid = rest.astype(BF16)
    low = (rest - mid.astype(F32)).astype(BF16)
    return high, mid, low


def remote(src, dst, send_sem, recv_sem, lon, lat):
    return pltpu.make_async_remote_copy(
        src_ref=src,
        dst_ref=dst,
        send_sem=send_sem,
        recv_sem=recv_sem,
        device_id={"lon": lon, "lat": lat},
        device_id_type=pl.DeviceIdType.MESH,
    )


def kernel(
    nlon,
    nlat,
    wet_hbm,
    east_hbm,
    north_hbm,
    cour_hbm,
    incr_hbm,
    innov_hbm,
    ow_hbm,
    scale_hbm,
    eta_ref,
    grad_ref,
    raw_i,
    raw_f,
    main,
    halo,
    work,
    delta,
    packed,
    strip_out,
    strip_in,
    corner,
    scale_buf,
    powers,
    gains,
    parts,
    sums,
    xbuf,
    zbuf,
    z_weight,
    known,
    in_sem,
    hs,
    hr,
    xs,
    xr,
    zs,
    zr,
):
    lon = lax.axis_index("lon")
    lat = lax.axis_index("lat")
    nz = nlon // XG
    x_pos = lax.rem(lon, XG)
    z_pos = lon // XG
    top = lat == nlat - 1
    low = lat == 0
    east_lon = lax.rem(lon + 1, nlon)
    west_lon = lax.rem(lon + nlon - 1, nlon)
    fold_lon = nlon - 1 - lon
    fold_ne = lax.rem(2 * nlon - 2 - lon, nlon)
    fold_nw = lax.rem(nlon - lon, nlon)
    ne_self = fold_ne == lon
    nw_self = fold_nw == lon

    loads = [
        pltpu.make_async_copy(scale_hbm, scale_buf, in_sem.at[7]),
        pltpu.make_async_copy(wet_hbm, raw_i.at[0], in_sem.at[0]),
        pltpu.make_async_copy(cour_hbm, raw_f.at[0], in_sem.at[1]),
        pltpu.make_async_copy(incr_hbm, raw_f.at[1], in_sem.at[2]),
        pltpu.make_async_copy(east_hbm, raw_i.at[1], in_sem.at[3]),
        pltpu.make_async_copy(north_hbm, raw_i.at[2], in_sem.at[4]),
        pltpu.make_async_copy(ow_hbm, main.at[4, pl.ds(PAD, 512)], in_sem.at[5]),
        pltpu.make_async_copy(innov_hbm, main.at[5, pl.ds(PAD, 512)], in_sem.at[6]),
    ]
    barrier = pltpu.get_barrier_semaphore()

    def greet(to_lon, to_lat):
        pl.semaphore_signal(
            barrier,
            inc=1,
            device_id={"lon": to_lon, "lat": to_lat},
            device_id_type=pl.DeviceIdType.MESH,
        )

    def x_peer(step):
        return z_pos * XG + lax.rem(x_pos + step, XG)

    def z_peer(step):
        return lax.rem(z_pos + step, nz) * XG + x_pos

    greet(east_lon, lat)
    greet(west_lon, lat)

    @pl.when(jnp.logical_not(low))
    def _():
        greet(lon, lat - 1)
        greet(east_lon, lat - 1)
        greet(west_lon, lat - 1)

    @pl.when(jnp.logical_not(top))
    def _():
        greet(lon, lat + 1)
        greet(east_lon, lat + 1)
        greet(west_lon, lat + 1)

    @pl.when(top)
    def _():
        greet(fold_lon, lat)

        @pl.when(jnp.logical_not(ne_self))
        def _():
            greet(fold_ne, lat)

        @pl.when(jnp.logical_not(nw_self))
        def _():
            greet(fold_nw, lat)

    for load in loads:
        load.start()
    far_first = sorted(range(1, nz), key=lambda step: -min(step, nz - step))
    for step in (1, nz - 1):
        greet(z_peer(step), lat)
    for step in range(1, XG):
        greet(x_peer(step), lat)

    lane8 = iota((8, 128), 1)
    sub8 = iota((8, 128), 0)

    zero8 = jnp.zeros((8, 128), F32)
    for block in range(4):
        for slot, side in ((0, 0), (6, 1), (7, 0), (7, 1)):
            strip_in[block, slot, side] = zero8
    for edge in (0, 536):
        for field in (0, 3):
            main[field, pl.ds(edge, 8)] = zero8
            halo[field, pl.ds(edge, 8)] = zero8
        work[0, pl.ds(edge, 8)] = zero8
        work[1, pl.ds(edge, 8)] = zero8

    @pl.when(low)
    def _():
        for field in range(FIELDS):
            main[field, pl.ds(8, 8)] = zero8
        corner[0] = zero8
        corner[1] = zero8

    for load in loads:
        load.wait()
    slot = (iota((32, 128), 1) + 8) // 16
    for block in range(4):
        for row in range(128 * block, 128 * block + 128, 32):
            rows, own = pl.ds(row, 32), pl.ds(row + PAD, 32)
            wet = raw_i[0, rows].astype(F32)
            fields = [
                wet * raw_f[1, rows],
                wet * raw_f[0, rows],
                raw_i[1, rows].astype(F32) * (1.0 / WLEV),
                raw_i[2, rows].astype(F32) * (1.0 / WLEV),
            ]
            for index, value in enumerate(fields):
                main[index, own] = value
            main[WEST, own] = roll(fields[2], 1, 1)
            fields.append(main[4, own])
            fields.append(main[5, own])
            joined = roll(fields[0], 16, 1)
            for index in range(1, FIELDS):
                moved = roll(fields[index], 16 * (index + 1), 1)
                joined = jnp.where(slot == index + 1, moved, joined)
            packed[rows] = joined

    links = 2 + (XG - 1) + 2
    north_links = jnp.where(
        top, 3 - ne_self.astype(jnp.int32) - nw_self.astype(jnp.int32), 3
    )
    south_links = jnp.where(low, 0, 3)
    pl.semaphore_wait(barrier, links + north_links + south_links)

    rounds = nz.bit_length() - 2

    def pass_on(index):
        for step in (2**index, nz - 2**index):
            pl.semaphore_signal(
                known.at[index],
                inc=1,
                device_id={"lon": z_peer(step), "lat": lat},
                device_id_type=pl.DeviceIdType.MESH,
            )

    def hear(index):
        pl.semaphore_wait(known.at[index], 2)
        if index + 1 < rounds:
            pass_on(index + 1)

    pass_on(0)

    top_rows = main.at[pl.ds(0, FIELDS), pl.ds(PAD + 504, 8)]
    low_rows = main.at[pl.ds(0, FIELDS), pl.ds(PAD, 8)]
    south_halo = main.at[pl.ds(0, FIELDS), pl.ds(8, 8)]
    north_halo = main.at[pl.ds(0, FIELDS), pl.ds(PAD + 512, 8)]
    top_tile = packed.at[pl.ds(504, 8)]
    low_tile = packed.at[pl.ds(0, 8)]
    to_west, to_east = [], []
    for block in range(4):
        first = strip_out.at[block, pl.ds(1, 6), 0], strip_in.at[block, pl.ds(1, 6), 0]
        last = strip_out.at[block, pl.ds(0, 6), 1], strip_in.at[block, pl.ds(0, 6), 1]
        to_west.append(remote(*first, hs.at[8 + block], hr.at[8 + block], west_lon, lat))
        to_east.append(remote(*last, hs.at[12 + block], hr.at[12 + block], east_lon, lat))
    to_south = remote(low_rows, north_halo, hs.at[0], hr.at[1], lon, lat - 1)
    to_sw = remote(low_tile, corner.at[3], hs.at[4], hr.at[7], west_lon, lat - 1)
    to_se = remote(low_tile, corner.at[2], hs.at[5], hr.at[6], east_lon, lat - 1)
    to_north = remote(top_rows, south_halo, hs.at[1], hr.at[0], lon, lat + 1)
    to_nw = remote(top_tile, corner.at[1], hs.at[6], hr.at[5], west_lon, lat + 1)
    to_ne = remote(top_tile, corner.at[0], hs.at[7], hr.at[4], east_lon, lat + 1)
    over_fold = remote(top_rows, north_halo, hs.at[1], hr.at[1], fold_lon, lat)
    fold_to_nw = remote(top_tile, corner.at[2], hs.at[6], hr.at[6], fold_nw, lat)
    fold_to_ne = remote(top_tile, corner.at[3], hs.at[7], hr.at[7], fold_ne, lat)
    own_nw = pltpu.make_async_copy(top_tile, corner.at[2], hr.at[6])
    own_ne = pltpu.make_async_copy(top_tile, corner.at[3], hr.at[7])

    @pl.when(top)
    def _():
        over_fold.start()

        @pl.when(jnp.logical_not(nw_self))
        def _():
            fold_to_nw.start()

        @pl.when(nw_self)
        def _():
            own_nw.start()

        @pl.when(jnp.logical_not(ne_self))
        def _():
            fold_to_ne.start()

        @pl.when(ne_self)
        def _():
            own_ne.start()

    @pl.when(jnp.logical_not(top))
    def _():
        to_north.start()
        to_nw.start()
        to_ne.start()

    @pl.when(jnp.logical_not(low))
    def _():
        to_south.start()
        to_sw.start()
        to_se.start()

    for block in range(4):
        turned = packed[pl.ds(128 * block, 128)].T
        strip_out[block] = turned.reshape(8, 2, 8, 128)
        to_west[block].start()
        to_east[block].start()

    scale = scale_buf[...]
    scale = jnp.concatenate([scale, scale], axis=0)
    stiff = scale * float(128 * 128)
    root_term = jnp.sqrt(1.0 + 4.0 * stiff)
    log_root = jnp.log1p(-(root_term - 1.0) / (2.0 * stiff))
    gain = (1.0 / root_term) * (2.0 * jnp.sqrt(jnp.sqrt(stiff)))
    both = jnp.where(sub8 < 4, log_root, gain)
    columns = jnp.concatenate([both] * 16, axis=0).T
    place = iota((128, 128), 1).astype(F32) - 63.5
    for block in range(4):
        rows = pl.ds(block * 128, 128)
        power = jnp.broadcast_to(columns[:, block : block + 1], (128, 128)) * place
        gain_rows = jnp.broadcast_to(columns[:, block + 4 : block + 5], (128, 128))
        up = jnp.exp(power)
        down = jnp.exp(-power)
        powers[rows, 0:128] = down
        powers[rows, 128:256] = up
        gains[rows, 0:128] = gain_rows * up
        gains[rows, 128:256] = gain_rows * down
    log_block = log_root * 128.0
    group_decay = jnp.exp(log_block * float(XG))
    image_sum = 1.0 - jnp.exp(log_block * float(nlon))

    for row in range(8, 536, RH):
        delta[0, pl.ds(row, RH)] = jnp.zeros((RH, 128), F32)
        delta[1, pl.ds(row, RH)] = jnp.zeros((RH, 128), F32)

    hear(0)

    first_half = lax.rem(lane8, 16) < 8
    def set_west(rows, outer):
        inner = main[WEST, rows]
        first = iota(inner.shape, 1) == 0
        main[WEST, rows] = jnp.where(first, outer, inner)
        halo[WEST, rows] = jnp.where(first, inner, outer)

    for block in range(4):
        own = pl.ds(128 * block + PAD, 128)
        to_west[block].wait_recv()
        to_east[block].wait_recv()
        edges = strip_in[block].reshape(128, 128).T
        for field in range(FIELDS):
            halo[field, own] = roll(edges, -16 * (field + 1), 1)
        set_west(own, roll(edges, 1 - 16 * 3, 1))

    @pl.when(jnp.logical_not(low))
    def _():
        to_north.wait_recv()
        to_nw.wait_recv()
        to_ne.wait_recv()

    south_corner = jnp.where(first_half, corner[1], corner[0])
    for field in range(FIELDS):
        halo[field, pl.ds(8, 8)] = roll(south_corner, -16 * (field + 1), 1)
    to_south.wait_recv()
    to_sw.wait_recv()
    to_se.wait_recv()

    @pl.when(top)
    def _():
        over_fold.wait_send()

    @pl.when(jnp.logical_not(top))
    def _():
        to_north.wait_send()

    @pl.when(jnp.logical_not(low))
    def _():
        to_south.wait_send()

    @pl.when(jnp.logical_not(top))
    def _():
        north_corner = jnp.where(first_half, corner[3], corner[2])
        for field in range(FIELDS):
            halo[field, pl.ds(PAD + 512, 8)] = roll(north_corner, -16 * (field + 1), 1)

    @pl.when(top)
    def _():
        mixed = jnp.where(first_half, corner[2], corner[3])
        tiles = [main[field, pl.ds(PAD + 512, 8)] for field in range(FIELDS)] + [mixed, zero8]
        stack = jnp.concatenate(tiles, axis=0)
        flip = (iota((128, 128), 0) + iota((128, 128), 1) == 127).astype(F32)
        row_to = iota((64, 64), 0)
        row_from = iota((64, 64), 1)
        swap = (row_to // 8 == row_from // 8) & (row_to % 8 + row_from % 8 == 7)
        turned = jnp.dot(stack, flip, precision=HIGH, preferred_element_type=F32)
        turned = jnp.dot(swap.astype(F32), turned, precision=HIGH, preferred_element_type=F32)
        ghost = pl.ds(PAD + 512, 8)
        for field in range(FIELDS):
            inner = turned[8 * field : 8 * field + 8]
            outer = roll(turned[48:56], 16 * (field + 1), 1)
            if field == 2:
                inner, outer = roll(inner, -1, 1), roll(outer, -1, 1)
                inner, outer = (
                    jnp.where(lane8 == 127, outer, inner),
                    jnp.where(lane8 == 127, inner, outer),
                )
            if field == 3:
                last = pl.ds(PAD + 504, 8)
                main[3, last] = jnp.where(sub8 == 7, main[3, last] * inner[0:1], main[3, last])
                halo[3, last] = jnp.where(sub8 == 7, halo[3, last] * outer[0:1], halo[3, last])
                inner, outer = roll(inner, -1, 0), roll(outer, -1, 0)
            main[field, ghost] = inner
            halo[field, ghost] = outer

    for edge in (8, PAD + 512):
        rows = pl.ds(edge, 8)
        main[WEST, rows] = roll(main[2, rows], 1, 1)
        set_west(rows, roll(halo[2, rows], 1, 1))

    last_lane = iota((RH, 128), 1) == 127
    zero_lane = iota((RH, 128), 1) == 0

    def substep(src, dst):
        for row in range(8, 536, RH):
            here, up, down = pl.ds(row, RH), pl.ds(row + 1, RH), pl.ds(row - 1, RH)
            states = [src[side][here] for side in range(2)]
            east = [roll(state, -1, 1) for state in states]
            west = [roll(state, 1, 1) for state in states]
            for side, field in enumerate((main, halo)[: 2 if dst else 1]):
                state = states[side]
                to_east = jnp.where(last_lane, east[1 - side], east[side]) - state
                to_west = jnp.where(zero_lane, west[1 - side], west[side]) - state
                spread = field[2, here] * to_east + field[WEST, here] * to_west
                spread = spread + field[3, here] * (src[side][up] - state)
                spread = spread + field[3, down] * (src[side][down] - state)
                change = delta[side, here] + field[1, here] * spread
                delta[side, here] = change
                if dst:
                    dst[side][here] = state + change

    side_a = (main.at[0], halo.at[0])
    side_b = (work.at[0], work.at[1])

    def forward_pair(step, carry):
        substep(side_a, side_b)
        substep(side_b, side_a)
        return carry

    lax.fori_loop(0, SUBSTEPS // 2, forward_pair, 0)

    for row in range(8, 536, RH):
        here = pl.ds(row, RH)
        for side, field in enumerate((main, halo)):
            height = field[0, here]
            start = field[1, here] * field[4, here] * (height - field[5, here])
            if side == 0:
                low_end, high_end = max(row, PAD), min(row + RH, PAD + 512)
                own = height[low_end - row : high_end - row]
                eta_ref[pl.ds(low_end - PAD, high_end - low_end)] = own
            work[side, here] = start
            delta[side, here] = start

    if rounds > 1:
        hear(1)

    def adjoint_pair(step, carry):
        substep(side_b, side_a)
        substep(side_a, side_b)
        return carry

    lax.fori_loop(0, SUBSTEPS // 2 - 1, adjoint_pair, 0)
    substep(side_b, side_a)
    substep(side_a, None)

    ends = jnp.zeros((8, 128), F32)
    pick_row = iota((8, 256), 0)
    pick_half = 4 * (iota((8, 256), 1) // 128)
    for block in range(4):
        rows = pl.ds(block * 128, 128)
        gradient = delta[0, pl.ds(PAD + block * 128, 128)] / raw_f[0, rows]
        both_ways = jnp.concatenate(
            [gradient * powers[rows, 0:128], gradient * powers[rows, 128:256]], axis=1
        )
        pick = (pick_row == pick_half + block).astype(BF16)
        for index, part in enumerate(split3(both_ways)):
            parts[index, rows] = part
            ends = ends + lax.dot_general(
                pick, part, (((1,), (1,)), ((), ())), preferred_element_type=F32
            )

    forward_half = sub8 < 4
    to_end, reach = [], []
    for step in range(XG):
        source = lax.rem(x_pos + XG - step, XG)
        blocks = jnp.where(forward_half, XG - 1 - source, source).astype(F32)
        to_end.append(jnp.exp(log_block * blocks))
        ahead = jnp.where(forward_half, x_pos - source, source - x_pos)
        near = jnp.exp(log_block * jnp.maximum(ahead, 1).astype(F32))
        reach.append(jnp.where(ahead > 0, near, 0.0))
    steps_in = jnp.where(forward_half, x_pos, XG - 1 - x_pos).astype(F32)
    group_weight = jnp.exp(log_block * (steps_in + 1.0)) / image_sum
    for step in range(1, nz + 1):
        z_weight[step - 1] = group_weight
        group_weight = group_weight * group_decay
    xbuf[0] = ends
    x_copies = [
        remote(xbuf.at[0], xbuf.at[step], xs.at[step - 1], xr.at[step - 1], x_peer(step), lat)
        for step in (2, 1, 3)
    ]
    for copy in x_copies:
        copy.start()

    for copy in x_copies:
        copy.wait_recv()
    tiles = [xbuf[step] for step in range(XG)]
    group = sum(to_end[step] * tiles[step] for step in range(XG))
    zbuf[0] = group
    z_copies = [
        remote(zbuf.at[0], zbuf.at[step], zs.at[step - 1], zr.at[step - 1], z_peer(step), lat)
        for step in far_first
    ]
    for index in range(2, rounds):
        hear(index)
    for copy in z_copies:
        copy.start()

    col = iota((256, 256), 1)
    row = iota((256, 256), 0)
    ahead = ((row < 128) & (col < 128) & (row <= col)) | ((row >= 128) & (col >= 128) & (row > col))
    ahead = ahead.astype(F32).astype(BF16)
    for block in range(4):
        rows = pl.ds(block * 128, 128)
        total = jnp.dot(parts[0, rows], ahead, preferred_element_type=F32)
        total = total + jnp.dot(parts[1, rows], ahead, preferred_element_type=F32)
        sums[rows] = total + jnp.dot(parts[2, rows], ahead, preferred_element_type=F32)

    inside = sum(reach[step] * tiles[step] for step in range(XG))
    for block in range(4):
        rows = pl.ds(block * 128, 128)
        both_gains = gains[rows]
        both_sums = both_gains * sums[rows]
        grad_ref[rows] = both_sums[:, 0:128] + both_sums[:, 128:256]

    for copy in z_copies:
        copy.wait_recv()
    terms = [inside]
    for step in range(1, nz + 1):
        tile = jnp.where(forward_half, zbuf[step % nz], zbuf[(nz - step) % nz])
        terms.append(z_weight[step - 1] * tile)
    while len(terms) > 1:
        terms = [a + b for a, b in zip(terms[::2], terms[1::2])] + terms[len(terms) // 2 * 2 :]
    inflow = terms[0]
    inflow_cols = jnp.concatenate([inflow] * 16, axis=0).T
    for block in range(4):
        rows = pl.ds(block * 128, 128)
        east_in = jnp.broadcast_to(inflow_cols[:, block : block + 1], (128, 128))
        west_in = jnp.broadcast_to(inflow_cols[:, block + 4 : block + 5], (128, 128))
        inner = gains[rows, 0:128] * east_in + gains[rows, 128:256] * west_in
        grad_ref[rows] = grad_ref[rows] + inner

    for copy in to_west + to_east:
        copy.wait_send()

    @pl.when(top)
    def _():
        @pl.when(jnp.logical_not(nw_self))
        def _():
            fold_to_nw.wait_send()

        @pl.when(jnp.logical_not(ne_self))
        def _():
            fold_to_ne.wait_send()

    @pl.when(jnp.logical_not(top))
    def _():
        to_nw.wait_send()
        to_ne.wait_send()

    @pl.when(jnp.logical_not(low))
    def _():
        to_sw.wait_send()
        to_se.wait_send()

    for copy in x_copies:
        copy.wait_send()
    for copy in z_copies:
        copy.wait_send()


def write_out(eta_ref, grad_ref, eta_hbm, grad_hbm, sem):
    copies = []
    for index, (src, dst) in enumerate(((eta_ref, eta_hbm), (grad_ref, grad_hbm))):
        for part in range(2):
            rows = pl.ds(part * 256, 256)
            copies.append(pltpu.make_async_copy(src.at[rows], dst.at[rows], sem.at[index, part]))
    for copy in copies:
        copy.start()
    for copy in copies:
        copy.wait()


def local(
    wet_mask, east_level, north_level, courant, increment, innovation, obs_weight, smooth_scale
):
    nlon = lax.axis_size("lon")
    nlat = lax.axis_size("lat")
    nz = nlon // XG
    inputs = (
        wet_mask,
        east_level,
        north_level,
        courant,
        increment,
        innovation,
        obs_weight,
        smooth_scale.reshape(4, 128),
    )
    hbm = pl.BlockSpec(memory_space=pltpu.MemorySpace.HBM)
    vmem = pl.BlockSpec(memory_space=pltpu.VMEM)
    dma = pltpu.SemaphoreType.DMA
    block = jax.ShapeDtypeStruct((512, 128), F32)
    eta, gradient = pl.pallas_call(
        functools.partial(kernel, nlon, nlat),
        out_shape=(block, block),
        in_specs=[hbm] * 8,
        out_specs=(vmem, vmem),
        scratch_shapes=[
            pltpu.VMEM((3, 512, 128), jnp.int32),
            pltpu.VMEM((2, 512, 128), F32),
            pltpu.VMEM((FIELDS + 1, 544, 128), F32),
            pltpu.VMEM((FIELDS + 1, 544, 128), F32),
            pltpu.VMEM((2, 544, 128), F32),
            pltpu.VMEM((2, 544, 128), F32),
            pltpu.VMEM((512, 128), F32),
            pltpu.VMEM((4, 8, 2, 8, 128), F32),
            pltpu.VMEM((4, 8, 2, 8, 128), F32),
            pltpu.VMEM((4, 8, 128), F32),
            pltpu.VMEM((4, 128), F32),
            pltpu.VMEM((512, 256), F32),
            pltpu.VMEM((512, 256), F32),
            pltpu.VMEM((3, 512, 256), BF16),
            pltpu.VMEM((512, 256), F32),
            pltpu.VMEM((XG, 8, 128), F32),
            pltpu.VMEM((nz, 8, 128), F32),
            pltpu.VMEM((nz, 8, 128), F32),
            pltpu.SemaphoreType.REGULAR((nz.bit_length() - 2,)),
            dma((8,)),
            dma((16,)),
            dma((16,)),
            dma((XG - 1,)),
            dma((XG - 1,)),
            dma((nz - 1,)),
            dma((nz - 1,)),
        ],
        compiler_params=pltpu.CompilerParams(
            collective_id=0, has_side_effects=True, vmem_limit_bytes=32 * 1024 * 1024
        ),
    )(*[pltpu.with_memory_space_constraint(value, pltpu.MemorySpace.HBM) for value in inputs])
    return pl.pallas_call(
        write_out,
        out_shape=(block, block),
        in_specs=[vmem] * 2,
        out_specs=(hbm, hbm),
        scratch_shapes=[dma((2, 2))],
        compiler_params=pltpu.CompilerParams(vmem_limit_bytes=1024 * 1024),
    )(eta, gradient)


def solution(mesh):
    return jax.shard_map(
        local,
        mesh=mesh,
        in_specs=(P("lat", "lon"),) * 7 + (P("lat"),),
        out_specs=(P("lat", "lon"), P("lat", "lon")),
        check_vma=False,
    )
```
